256 devices in a mesh: lst: 8 (over y, core), chan: 32 (over x, z).
Axes of the slice: x: 4, y: 4, z: 8, core: 2. Of those that a mesh axis runs over, the one named last changes fastest.
Arguments:
- visibility: bfloat16 [2, 8, 2048, 8, 1536], P(None, 'lst', None, None, 'chan'), may hold values from -6 to 6
- inverse_cov: bfloat16 [1536, 1536], replicated, as said below
- group_size: int32 [2048], replicated, may hold values from 2 to 8, as said below
- group_owner: int32 [2048], replicated, may hold values from 0 to 2047, each once
- lst_bin: int32 [8], P('lst'), may hold values from 0 to 7
Outputs:
- power: float32 [8, 2048, 1536], P(None, 'chan', 'lst')
The draws below stay inside these ranges and needn't reach their ends.
Inputs may be any that keep to these rules, and one draw needn't show every extreme that they name: `inverse_cov`: symmetric and positive definite. `group_size`: some group has exactly 8 live baselines; slots at or past a group's size are padding. `group_owner`: each position 0 to 2047 appears once.
All inputs are finite; a program needn't handle non-finite values.
Results may differ from the reference program's by a relative error of at most 0.0057.
Values may be sent and summed in bfloat16 or wider, within the bound.
A program may use at most 128 MiB of HBM per device.

```python
import math
import jax
import jax.numpy as jnp
from jax import lax

F = 1536
SLOT = 8
NBIN = 8
TIMES = 8
GROUPS = 2048


def draw_inverse_cov(key, part):
    noise = jax.random.normal(jax.random.fold_in(key, 11), (F, F), jnp.float32)
    symmetric = (noise + noise.T) * (0.3 / math.sqrt(F))
    return (jnp.eye(F, dtype=jnp.float32) + symmetric).astype(jnp.bfloat16)


def draw_group_size(key, part):
    first_key, second_key = jax.random.split(jax.random.fold_in(key, 23))
    drawn_sizes = jax.random.randint(first_key, (GROUPS,), 2, SLOT + 1)
    full_group = jax.random.randint(second_key, (), 0, GROUPS)
    return jnp.where(jnp.arange(GROUPS) == full_group, SLOT, drawn_sizes).astype(jnp.int32)


def set_ends(entries, rng, least, top_value):
    longest = entries.shape.index(max(entries.shape))
    spots = []
    for shift in (0, 1):
        where = [jax.random.randint(jax.random.fold_in(rng, axis), (), 0, length) for axis, length in enumerate(entries.shape)]
        where[longest] = (where[longest] + shift) % entries.shape[longest]
        spots.append(tuple(where))
    return entries.at[spots[0]].set(least).at[spots[1]].set(top_value)


def levels(stream_key, shape, cuts, least, high):
    gain = 1.0
    for axis_at, parts in cuts:
        draws = jax.random.uniform(jax.random.fold_in(jax.random.fold_in(stream_key, 6), axis_at), (parts,), jnp.float32, least / len(cuts), high / len(cuts))
        gain = gain * jnp.repeat(jnp.exp(draws), shape[axis_at] // parts).reshape((-1,) + (1,) * (len(shape) - 1 - axis_at))
    return gain


def gaussian(own_key, dims, scale, limit, shards=(), kind=jnp.bfloat16):
    gain = levels(own_key, dims, shards, -0.22, 0.18) if shards else 1.0
    entries = jax.random.normal(own_key, dims, jnp.float32) * scale * gain
    return jnp.minimum(jnp.maximum(entries, -limit), limit).astype(kind)


def setup_inputs(seed: int = 0) -> dict:
    splits = jax.random.split(jax.random.key(seed), 6)
    visibility = gaussian(splits[0], (2, TIMES, GROUPS, SLOT, F), 1.0, 6.0, ((1, 8), (4, 32)))
    inverse_cov = draw_inverse_cov(jax.random.fold_in(splits[5], 71), 0)
    group_size = draw_group_size(jax.random.fold_in(splits[5], 71), 0)
    group_owner = jax.random.permutation(splits[3], GROUPS).astype(jnp.int32)
    lst_bin = set_ends(jax.random.randint(splits[4], (TIMES,), 0, NBIN), jax.random.fold_in(splits[4], 1), 0, NBIN - 1).astype(jnp.int32)
    return dict(visibility=visibility, inverse_cov=inverse_cov, group_size=group_size, group_owner=group_owner, lst_bin=lst_bin)


def delay_tables(channels):
    channel_index = jnp.arange(channels, dtype=jnp.int32)
    phase_index = channel_index[:, None] * channel_index[None, :] % channels
    angles = 2.0 * math.pi / channels * phase_index.astype(jnp.float32)
    base_angle = 2.0 * math.pi / channels * channel_index.astype(jnp.float32)
    window_taper = 0.35875 - 0.48829 * jnp.cos(base_angle) + 0.14128 * jnp.cos(2.0 * base_angle) - 0.01168 * jnp.cos(3.0 * base_angle)
    column_scale = window_taper[:, None] * (2.0 / math.sqrt(channels))
    return ((column_scale * jnp.cos(angles)).astype(jnp.bfloat16), (column_scale * jnp.sin(angles)).astype(jnp.bfloat16))

def pair_power(regrouped, live_sizes, inverse_cov, tables):
    cos_table, sin_table = tables
    time_count, group_count, slot_count, channels = (regrouped.shape[1], regrouped.shape[2], regrouped.shape[3], regrouped.shape[4])
    row_count = time_count * group_count * slot_count
    flat_rows = regrouped.reshape(2 * row_count, channels)
    weighted = jnp.dot(flat_rows, inverse_cov, preferred_element_type=jnp.float32).astype(jnp.bfloat16)
    joined_table = jnp.concatenate([cos_table, sin_table], axis=1)
    product = jnp.dot(weighted, joined_table, preferred_element_type=jnp.float32)
    real_cos = product[:row_count, :channels]
    real_sin = product[:row_count, channels:]
    imag_cos = product[row_count:, :channels]
    imag_sin = product[row_count:, channels:]
    grid_shape = (time_count, group_count, slot_count, channels)
    delay_real = (real_cos + imag_sin).reshape(grid_shape)
    delay_imag = (imag_cos - real_sin).reshape(grid_shape)
    live_mask = (jnp.arange(slot_count, dtype=jnp.int32)[None, :] < live_sizes[:, None]).astype(jnp.float32)[None, :, :, None]
    summed_real = lax.optimization_barrier(jnp.sum(delay_real * live_mask, axis=2))
    summed_imag = lax.optimization_barrier(jnp.sum(delay_imag * live_mask, axis=2))
    self_power = lax.optimization_barrier(jnp.sum((delay_real * delay_real + delay_imag * delay_imag) * live_mask, axis=2))
    members = live_sizes.astype(jnp.float32)
    pair_count = members * (members - 1.0)
    return (summed_real * summed_real + summed_imag * summed_imag - self_power) / pair_count[None, :, None]

def bin_power(crossed, bin_index):
    binned = []
    for which_bin in range(NBIN):
        selected = (bin_index == which_bin).astype(jnp.float32)[:, None, None]
        binned.append(lax.optimization_barrier(jnp.sum(crossed * selected, axis=0)))
    return jnp.stack(binned, axis=0)

def reference(visibility, inverse_cov, group_size, group_owner, lst_bin):
    owner_order = jnp.argsort(group_owner).astype(jnp.int32)
    regrouped = jnp.take(visibility, owner_order, axis=2)
    live_sizes = jnp.take(group_size, owner_order)
    tables = delay_tables(F)
    frames = jnp.moveaxis(regrouped, 1, 0)[:, :, None]
    crossed = lax.map(lambda one_frame: pair_power(one_frame, live_sizes, inverse_cov, tables), frames)
    crossed = crossed.reshape(TIMES, GROUPS, F)
    summed = bin_power(crossed, lst_bin)
    onehot = (lst_bin[:, None] == jnp.arange(NBIN, dtype=jnp.int32)[None, :]).astype(jnp.float32)
    counts = lax.optimization_barrier(jnp.sum(onehot, axis=0))
    return summed / jnp.maximum(counts, 1.0)[:, None, None]
```

```python
import functools
import math

import jax
import jax.numpy as jnp
from jax import lax
from jax.experimental import pallas as pl
from jax.experimental.pallas import tpu as pltpu
from jax.sharding import PartitionSpec as P

NBIN = 8
SLOT = 8
MESH = pl.DeviceIdType.MESH
F32 = jnp.float32
BF16 = jnp.bfloat16
NN = (((1,), (0,)), ((), ()))
NT = (((1,), (1,)), ((), ()))
TN = (((0,), (0,)), ((), ()))
ORDER = ((4, 3, 5, 0), (2, 6, 1, 7))
TAIL = 16


def dot(a, b, dims=NN):
    return lax.dot_general(a, b, dims, preferred_element_type=F32)


def one_if(condition):
    return jnp.where(condition, 1.0, 0.0).astype(BF16)


def kernel(
    cap,
    sizes,
    bin_ref,
    owner_ref,
    size_ref,
    vis_ref,
    cov_hbm,
    out_ref,
    cov,
    gathered,
    paired,
    send,
    rows,
    table,
    fold,
    acc,
    step_cos,
    step_sin,
    base_cos,
    base_sin,
    member,
    plus,
    minus,
    landed,
    bin_send,
    bin_land,
    cov_sem,
    own_sem,
    send_sem,
    recv_sem,
    y_send,
    y_recv,
    b_send,
    b_recv,
):
    nx, nz, nl, held, channels, width = sizes
    half = channels // 2
    part = channels // nl
    lst = lax.axis_index("lst")
    chan = lax.axis_index("chan")
    x, z = chan // nz, chan % nz
    quads = nx * nz // 4
    per_x = nz // 4

    def place(q, i):
        dz = ORDER[0][i] + (q % per_x) * (ORDER[1][i] - ORDER[0][i])
        return lax.rem(x + q // per_x, nx) * nz + lax.rem(z + dz, nz)

    def landing():
        return rows.at[pl.ds(pl.multiple_of(chan * width, 16), width), :]

    def block_copy(q, i):
        n = 4 * q + i
        return pltpu.make_async_remote_copy(
            src_ref=send.at[n],
            dst_ref=landing(),
            send_sem=send_sem.at[n],
            recv_sem=recv_sem.at[n],
            device_id=(lst, place(q, i)),
            device_id_type=MESH,
        )

    own_copy = pltpu.make_async_copy(send.at[3], landing(), own_sem)
    cov_copy = pltpu.make_async_copy(cov_hbm, cov, cov_sem)

    barrier = pltpu.get_barrier_semaphore()
    for other in range(1, nx * nz):
        peer = lax.rem(x + other // nz, nx) * nz + lax.rem(z + other % nz, nz)
        pl.semaphore_signal(barrier, inc=1, device_id=(lst, peer), device_id_type=MESH)
    for dl in range(1, nl):
        pl.semaphore_signal(
            barrier, inc=1, device_id=(lax.rem(lst + dl, nl), chan), device_id_type=MESH
        )
    cov_copy.start()
    bin_send[...] = jnp.full(bin_send.shape, bin_ref[0], jnp.int32).astype(F32).astype(BF16)
    plus[pl.ds(half, TAIL), :] = jnp.zeros((TAIL, held), BF16)

    low = lax.broadcasted_iota(jnp.int32, (width, 2 * held), 1) < held
    rank = lax.broadcasted_iota(jnp.int32, (held, cap), 1)
    spot = lax.broadcasted_iota(jnp.int32, (4 * held, 1), 0)

    def quad(q, first):
        base = jnp.zeros((4 * held, 1), jnp.int32)
        for i in range(4):
            here = (spot >= i * held) & (spot < (i + 1) * held)
            base = jnp.where(here, place(q, i) * held - i * held, base)
        hit = owner_ref[...] == base + spot
        live = jnp.sum(jnp.where(hit, size_ref[...], 0), axis=1, keepdims=True)
        row_id = lax.broadcasted_iota(jnp.int32, (4 * held, 4 * held), 0)
        col_id = lax.broadcasted_iota(jnp.int32, (4 * held, 4 * held), 1)
        before = one_if((row_id // held == col_id // held) & (col_id < row_id))
        live_wide = jnp.broadcast_to(live.astype(F32), (4 * held, 128)).astype(BF16)
        start = dot(before, live_wide)[:, :1].astype(jnp.int32)
        gathered[...] = dot(vis_ref[...], one_if(hit), NT)
        for i in range(4):
            for c in range(2):
                for pair in range(SLOT // 2):
                    r0 = (c * SLOT + 2 * pair) * width
                    lanes = pl.ds((i // 2) * 2 * held, 2 * held)
                    left = gathered[pl.ds(r0, width), lanes]
                    right = gathered[pl.ds(r0 + width, width), lanes]
                    if i % 2 == 0:
                        joined = jnp.where(low, left, pltpu.roll(right, held, 1))
                    else:
                        joined = jnp.where(low, pltpu.roll(left, held, 1), right)
                    paired[i, pl.ds(c * width, width), pl.ds(pair * 2 * held, 2 * held)] = (
                        joined.astype(BF16)
                    )
        for i in range(4):
            live_i = live[i * held : (i + 1) * held]
            start_i = start[i * held : (i + 1) * held]
            chosen = [
                one_if(rank == jnp.where(live_i > s, start_i + s, -1)) for s in range(SLOT)
            ]
            block = dot(paired[i], jnp.concatenate(chosen, axis=0)).astype(BF16)
            send[4 * q + i, :, pl.ds(0, cap)] = block[:width]
            send[4 * q + i, :, pl.ds(cap, cap)] = block[width:]
            if i > 0:
                if first and i == 1:
                    pl.semaphore_wait(barrier, nx * nz - 1 + nl - 1)
                block_copy(q, i - 1).start()
            elif not first:

                @pl.when(q > 1)
                def _():
                    block_copy(q - 1, 3).start()

                @pl.when(q == 1)
                def _():
                    own_copy.start()

            if first and i == 3:
                member[...] = one_if((rank >= start_i) & (rank < start_i + live_i))

    quad(0, True)

    def later(q, carry):
        quad(q, False)
        return carry

    lax.fori_loop(1, quads, later, 0)
    block_copy(quads - 1, 3).start()

    def bin_copy(dl):
        return pltpu.make_async_remote_copy(
            src_ref=bin_send,
            dst_ref=bin_land.at[lst],
            send_sem=b_send.at[dl],
            recv_sem=b_recv.at[dl],
            device_id=(lax.rem(lst + dl, nl), chan),
            device_id_type=MESH,
        )

    for dl in range(1, nl):
        bin_copy(dl).start()
    bin_land[lst] = bin_send[...]

    steps = step_cos.shape[0]
    bases = half // steps
    unit = 2.0 * math.pi / channels

    def phase(k, f):
        product = k * f
        turns = jnp.floor(product * (1.0 / channels))
        return (product - turns * channels) * unit

    def grid(shape, dim):
        return lax.broadcasted_iota(jnp.int32, shape, dim).astype(F32)

    shape = (steps, channels)
    angle = phase(grid(shape, 0), grid(shape, 1))
    step_cos[...] = jnp.cos(angle)
    step_sin[...] = jnp.sin(angle)
    shape = (base_cos.shape[0], channels)
    angle = grid(shape, 1) * unit
    taper = (
        0.35875
        - 0.48829 * jnp.cos(angle)
        + 0.14128 * jnp.cos(2.0 * angle)
        - 0.01168 * jnp.cos(3.0 * angle)
    ) * (2.0 / math.sqrt(channels))
    angle = phase(grid(shape, 0) * float(steps), grid(shape, 1))
    base_cos[...] = taper * jnp.cos(angle)
    base_sin[...] = taper * jnp.sin(angle)
    channel = lax.broadcasted_iota(jnp.int32, (1, channels), 1)
    middle = taper[:1] * jnp.where(channel % 2 == 0, 1.0, -1.0)
    step_row = lax.broadcasted_iota(jnp.int32, (steps, channels), 0)

    def tables(a, carry):
        bc, bs = base_cos[pl.ds(a, 1), :], base_sin[pl.ds(a, 1), :]
        uc, us = step_cos[...], step_sin[...]
        at = pl.multiple_of(a * steps, steps)
        table[pl.ds(at, steps), :] = (uc * bc - us * bs).astype(BF16)
        sines = jnp.where(step_row + at == 0, middle, us * bc + uc * bs)
        table[pl.ds(half + at, steps), :] = sines.astype(BF16)
        return carry

    lax.fori_loop(0, bases, tables, 0)
    cov_copy.wait()
    tall = 256

    def folding(i, carry):
        at = pl.ds(pl.multiple_of(i * tall, tall), tall)
        fold[at, :] = dot(table[at, :], cov[...]).astype(BF16)
        return carry

    lax.fori_loop(0, channels // tall, folding, 0)
    own_copy.wait()

    def arrive(q):
        for i in range(4):

            @pl.when(4 * q + i != 3)
            def _():
                block_copy(q, i).wait_recv()

    deep = nz * width

    def group(g, carry):
        for odd in range(per_x):
            arrive(per_x * g + odd)
        from_x = lax.rem(x + nx - g, nx)
        ch = pl.ds(pl.multiple_of(from_x * deep, deep), deep)

        def strip(i, inner):
            at = pl.ds(pl.multiple_of(i * tall, tall), tall)
            part_sum = dot(fold[at, ch], rows[ch, :])

            @pl.when(g == 0)
            def _():
                acc[at, :] = part_sum

            @pl.when(g > 0)
            def _():
                acc[at, :] += part_sum

            return inner

        return lax.fori_loop(0, channels // tall, strip, carry)

    lax.fori_loop(0, nx, group, 0)

    members = dot(jnp.ones((8, cap), BF16), member[...], NT)[:1]
    scale = 1.0 / (members * (members - 1.0))

    def share_copy(source, h, to, dl):
        return pltpu.make_async_remote_copy(
            src_ref=source.at[pl.ds(pl.multiple_of(h * part, 16), part + TAIL), :],
            dst_ref=landed.at[lst],
            send_sem=y_send.at[to],
            recv_sem=y_recv.at[dl],
            device_id=(to, chan),
            device_id_type=MESH,
        )

    def share(source, h, to):
        @pl.when(to != lst)
        def _():
            share_copy(source, h, to, lax.rem(to - lst + nl, nl)).start()

        @pl.when(to == lst)
        def _():
            landed[lst] = source[pl.ds(pl.multiple_of(h * part, 16), part + TAIL), :]

    def finish(h, carry):
        at = pl.multiple_of(h * part, part)
        rc = acc[pl.ds(at, part), pl.ds(0, cap)]
        ic = acc[pl.ds(at, part), pl.ds(cap, cap)]
        rs = acc[pl.ds(half + at, part), pl.ds(0, cap)]
        im = acc[pl.ds(half + at, part), pl.ds(cap, cap)]
        ends = lax.broadcasted_iota(jnp.int32, (part, 1), 0) + at == 0
        even = rc * rc + ic * ic
        odd = rs * rs + im * im
        cross = 2.0 * (rc * im - ic * rs)
        power_plus = jnp.where(ends, even, even + odd + cross).astype(BF16)
        power_minus = jnp.where(ends, odd, even + odd - cross).astype(BF16)
        mine = member[...]

        def total(v):
            return dot(v, mine, NT)

        def exact(v):
            head = v.astype(BF16)
            return total(head) + total((v - head.astype(F32)).astype(BF16))

        src, sic = exact(rc), exact(ic)
        srs, sim = exact(rs), exact(im)
        zero = jnp.zeros_like(src)
        a, b = jnp.where(ends, src, src + sim), jnp.where(ends, sic, sic - srs)
        plus[pl.ds(at, part), :] = ((a * a + b * b - total(power_plus)) * scale).astype(BF16)
        a, b = jnp.where(ends, srs, src - sim), jnp.where(ends, sim, sic + srs)
        under = ((a * a + b * b - total(power_minus)) * scale).astype(BF16)
        minus[pl.ds(at, part), :] = under

        @pl.when(h == 0)
        def _():
            minus[pl.ds(half, TAIL), :] = under[:TAIL]

        @pl.when(h > 0)
        def _():
            share(plus, h - 1, h - 1)
            share(minus, h - 1, nl - h)

        return carry

    spans = half // part
    lax.fori_loop(0, spans, finish, 0)
    share(plus, spans - 1, spans - 1)
    share(minus, spans - 1, nl - spans)

    for dl in range(1, nl):
        bin_copy(dl).wait()
        share_copy(plus, 0, lax.rem(lst + dl, nl), dl).wait_recv()
    row = lax.broadcasted_iota(jnp.int32, (part + TAIL, part), 0)
    col = lax.broadcasted_iota(jnp.int32, (part + TAIL, part), 1)
    turn = one_if(row == jnp.where(lst < spans, col, part - col))
    for t in range(nl):
        piece = dot(landed[t], turn, TN)
        code = bin_land[t].astype(F32)[:1, :1]
        for b in range(NBIN):
            term = jnp.where(code == b, piece, 0.0)
            if t == 0:
                out_ref[b] = term
            else:
                out_ref[b] += term
    for b in range(NBIN):
        count = jnp.zeros((1, 1), F32)
        for t in range(nl):
            count += jnp.where(bin_land[t].astype(F32)[:1, :1] == b, 1.0, 0.0)
        out_ref[b] = out_ref[b] / jnp.maximum(count, 1.0)

    def sent(q, carry):
        for i in range(4):

            @pl.when(4 * q + i != 3)
            def _():
                block_copy(q, i).wait_send()

        return carry

    lax.fori_loop(0, quads, sent, 0)
    for dl in range(1, nl):
        to = lax.rem(lst + dl, nl)
        share_copy(plus, 0, to, dl).wait_send()


def cross_power(cap, collective_id, sizes, lst_bin, owner, size, vis, cov):
    nx, nz, nl, held, channels, width = sizes
    half = channels // 2
    part = channels // nl
    total = nx * nz
    vmem = pltpu.VMEM
    dma = pltpu.SemaphoreType.DMA
    return pl.pallas_call(
        functools.partial(kernel, cap, sizes),
        out_shape=jax.ShapeDtypeStruct((NBIN, held, part), F32),
        in_specs=[
            pl.BlockSpec(memory_space=pltpu.SMEM),
            pl.BlockSpec(memory_space=vmem),
            pl.BlockSpec(memory_space=vmem),
            pl.BlockSpec(memory_space=vmem),
            pl.BlockSpec(memory_space=pl.ANY),
        ],
        out_specs=pl.BlockSpec(memory_space=vmem),
        scratch_shapes=[
            vmem((channels, channels), BF16),
            vmem((2 * SLOT * width, 4 * held), F32),
            vmem((4, 2 * width, SLOT * held), BF16),
            vmem((total, width, 2 * cap), BF16),
            vmem((channels, 2 * cap), BF16),
            vmem((channels, channels), BF16),
            vmem((channels, channels), BF16),
            vmem((channels, 2 * cap), F32),
            vmem((64, channels), F32),
            vmem((64, channels), F32),
            vmem((16, channels), F32),
            vmem((16, channels), F32),
            vmem((held, cap), BF16),
            vmem((half + TAIL, held), BF16),
            vmem((half + TAIL, held), BF16),
            vmem((nl, part + TAIL, held), BF16),
            vmem((16, 128), BF16),
            vmem((nl, 16, 128), BF16),
            dma(()),
            dma(()),
            dma((total,)),
            dma((total,)),
            dma((nl,)),
            dma((nl,)),
            dma((nl,)),
            dma((nl,)),
        ],
        compiler_params=pltpu.CompilerParams(
            collective_id=collective_id, has_side_effects=True, vmem_limit_bytes=60 * 2**20
        ),
    )(lst_bin, owner, size, vis, cov)


def solution(mesh):
    nl, total = mesh.shape["lst"], mesh.shape["chan"]
    nx = total // 8
    nz = total // nx

    def shards(visibility, inverse_cov, group_size, group_owner, lst_bin):
        groups, width = visibility.shape[2], visibility.shape[4]
        channels = inverse_cov.shape[0]
        held = groups // total
        sizes = (nx, nz, nl, held, channels, width)
        vis = jnp.transpose(visibility, (0, 1, 3, 4, 2)).reshape(2 * SLOT * width, groups)
        owner = group_owner.reshape(1, groups)
        size = group_size.reshape(1, groups)
        home = group_owner[None, :] // held == jnp.arange(total, dtype=jnp.int32)[:, None]
        most = jnp.max(jnp.sum(jnp.where(home, size, 0), axis=1))
        full = SLOT * held
        tight = full * 3 // 4
        return lax.cond(
            most <= tight,
            functools.partial(cross_power, tight, 0, sizes),
            functools.partial(cross_power, full, 1, sizes),
            lst_bin, owner, size, vis, inverse_cov,
        )

    placed = (P(None, "lst", None, None, "chan"), P(), P(), P(), P("lst"))
    return jax.shard_map(
        shards, mesh=mesh, in_specs=placed, out_specs=P(None, "chan", "lst"), check_vma=False
    )
```

```python
import functools
import math

import jax
import jax.numpy as jnp
from jax import lax
from jax.experimental import pallas as pl
from jax.experimental.pallas import tpu as pltpu
from jax.sharding import PartitionSpec as P

NBIN = 8
SLOT = 8
MESH = pl.DeviceIdType.MESH
F32 = jnp.float32
BF16 = jnp.bfloat16
NN = (((1,), (0,)), ((), ()))
NT = (((1,), (1,)), ((), ()))
TN = (((0,), (0,)), ((), ()))
TAIL = 16
LANES = 128


def dot(a, b, dims=NN):
    return lax.dot_general(a, b, dims, preferred_element_type=F32)


def one_if(condition):
    return jnp.where(condition, 1.0, 0.0).astype(BF16)


def fits_kernel(base, room, sizes, owner_ref, size_ref, out_ref):
    nx, nz, nl, held, channels, width = sizes
    first = lax.broadcasted_iota(jnp.int32, (nx * nz, 1), 0) * held
    owner = owner_ref[...]
    mine = (owner >= first) & (owner < first + held)
    lives = jnp.sum(jnp.where(mine, size_ref[...], 0), axis=1, keepdims=True)
    over = jnp.maximum(lives - base, 0).reshape(nx, nz, 1)
    out_ref[0] = jnp.where(jnp.max(jnp.sum(over, axis=0)) <= room, 1, 0)


def kernel(
    cap,
    sizes,
    bin_ref,
    owner_ref,
    size_ref,
    vis_ref,
    cov_hbm,
    out_ref,
    cov,
    pick,
    chosen,
    gathered,
    paired,
    send_a,
    send_b,
    send_p,
    rows_a,
    rows_b,
    rows_p,
    table,
    fold,
    step_cos,
    step_sin,
    base_cos,
    base_sin,
    member_a,
    member_b,
    member_p,
    scale_ref,
    sums,
    share_plus,
    share_minus,
    landed,
    pieces,
    bin_send,
    bin_land,
    cov_sem,
    own_sem,
    a_send,
    a_recv,
    b_send,
    b_recv,
    p_send,
    p_recv,
    f_send,
    f_recv,
    y_send,
    y_recv,
    n_send,
    n_recv,
):
    nx, nz, nl, held, channels, width = sizes
    half = channels // 2
    part = channels // nl
    spans = half // part
    base = cap + held
    wide = cap + 2 * LANES
    lst = lax.axis_index("lst")
    chan = lax.axis_index("chan")
    x, z = chan // nz, chan % nz
    last = nz - 1

    def ahead(q):
        return nz // 2 + (1 - 2 * (q % 2)) * ((q + 1) // 2)

    def place(q, i):
        return lax.rem(x + i, nx) * nz + lax.rem(z + ahead(q), nz)

    def rows_of(ref, source):
        return ref.at[pl.ds(pl.multiple_of(source * width, 16), width), :]

    def a_copy(q, i):
        n = nx * q + i
        return pltpu.make_async_remote_copy(
            src_ref=send_a.at[n],
            dst_ref=rows_of(rows_a, chan),
            send_sem=a_send.at[n],
            recv_sem=a_recv.at[n],
            device_id=(lst, place(q, i)),
            device_id_type=MESH,
        )

    def b_copy(q, i):
        n = nx * q + i
        return pltpu.make_async_remote_copy(
            src_ref=send_b.at[n],
            dst_ref=rows_of(rows_b, chan),
            send_sem=b_send.at[n],
            recv_sem=b_recv.at[n],
            device_id=(lst, place(q, i)),
            device_id_type=MESH,
        )

    def p_copy(q):
        return pltpu.make_async_remote_copy(
            src_ref=send_p.at[q],
            dst_ref=rows_of(rows_p, chan),
            send_sem=p_send.at[q],
            recv_sem=p_recv.at[q],
            device_id=(lst, place(q, 0)),
            device_id_type=MESH,
        )

    def f_copy(q, j):
        source = x * nz + lax.rem(z + nz - ahead(q), nz)
        n = (nx - 1) * q + j - 1
        return pltpu.make_async_remote_copy(
            src_ref=rows_of(rows_p, source),
            dst_ref=rows_of(rows_p, source),
            send_sem=f_send.at[n],
            recv_sem=f_recv.at[n],
            device_id=(lst, lax.rem(x + j, nx) * nz + z),
            device_id_type=MESH,
        )

    own_a = pltpu.make_async_copy(send_a.at[nx * last], rows_of(rows_a, chan), own_sem.at[0])
    own_b = pltpu.make_async_copy(send_b.at[nx * last], rows_of(rows_b, chan), own_sem.at[1])
    own_p = pltpu.make_async_copy(send_p.at[last], rows_of(rows_p, chan), own_sem.at[2])
    cov_copy = pltpu.make_async_copy(cov_hbm, cov, cov_sem)

    barrier = pltpu.get_barrier_semaphore()
    for other in range(1, nx * nz):
        peer = lax.rem(x + other // nz, nx) * nz + lax.rem(z + other % nz, nz)
        pl.semaphore_signal(barrier, inc=1, device_id=(lst, peer), device_id_type=MESH)
    for dl in range(1, nl):
        pl.semaphore_signal(
            barrier, inc=1, device_id=(lax.rem(lst + dl, nl), chan), device_id_type=MESH
        )
    cov_copy.start()

    low = lax.broadcasted_iota(jnp.int32, (width, LANES), 1) < held
    lane = lax.broadcasted_iota(jnp.int32, (1, wide), 1)
    spot = lax.broadcasted_iota(jnp.int32, (held, LANES), 0).astype(F32).astype(BF16)
    row_id = lax.broadcasted_iota(jnp.int32, (nx * held, nx * held), 0)
    col_id = lax.broadcasted_iota(jnp.int32, (nx * held, nx * held), 1)
    before = one_if((row_id // held == col_id // held) & (col_id < row_id))
    one, none = jnp.ones((held, LANES), BF16), jnp.zeros((held, LANES), BF16)

    def members(start, live, pooled):
        at = lax.broadcasted_iota(jnp.int32, (held, cap), 1)
        mine = one_if((at >= start) & (at < start + live))
        empty = jnp.zeros((held, cap), BF16)
        member_a[pl.ds(0, held), :] = jnp.concatenate([mine, empty], axis=1)
        member_a[pl.ds(held, held), :] = jnp.concatenate([empty, mine], axis=1)
        at = lax.broadcasted_iota(jnp.int32, (held, LANES), 1)
        below = at < held
        near = lax.rem(at, held) + cap
        mine = (near >= start) & (near < start + live)
        member_b[pl.ds(0, held), :] = one_if(mine & below)
        member_b[pl.ds(held, held), :] = one_if(mine & jnp.logical_not(below))
        far = at + base - pooled
        mine = one_if((far >= jnp.maximum(start, base)) & (far < start + live))
        empty = jnp.zeros((held, LANES), BF16)
        member_p[pl.ds(0, held), :] = jnp.concatenate([mine, empty], axis=1)
        member_p[pl.ds(held, held), :] = jnp.concatenate([empty, mine], axis=1)
        row_id = lax.broadcasted_iota(jnp.int32, (held, LANES), 0)
        lane = lax.rem(lax.broadcasted_iota(jnp.int32, (held, LANES), 1), held)
        spread = jnp.where(row_id == lane, jnp.broadcast_to(live, (held, LANES)), 0)
        count = jnp.sum(spread.astype(F32), axis=0, keepdims=True)
        scale_ref[...] = jnp.broadcast_to(1.0 / (count * (count - 1.0)), scale_ref.shape)

    def column(q, first):
        groups = owner_ref.shape[1]
        lives = []
        for i in range(nx):
            seat = owner_ref[...] - place(q, i) * held
            seat = jnp.where((seat >= 0) & (seat < held), seat, -1).astype(F32).astype(BF16)
            sized = size_ref[...].astype(F32).astype(BF16)
            live_sum = none
            for g in range(0, groups, LANES):
                hit = jnp.broadcast_to(seat[:, g : g + LANES], (held, LANES)) == spot
                pick[pl.ds(i * held, held), pl.ds(g, LANES)] = jnp.where(hit, one, none)
                sizes_here = jnp.broadcast_to(sized[:, g : g + LANES], (held, LANES))
                live_sum += jnp.where(hit, sizes_here, none)
            lives.append(jnp.sum(live_sum.astype(F32), axis=1, keepdims=True))
        live = jnp.concatenate(lives, axis=0)
        live_wide = jnp.broadcast_to(live, (nx * held, LANES)).astype(BF16)
        start = dot(before, live_wide)[:, :1].astype(jnp.int32)
        live = live.astype(jnp.int32)
        gathered[...] = dot(vis_ref[...], pick[...], NT)
        for i in range(nx):
            for c in range(2):
                for pair in range(SLOT // 2):
                    r0 = (c * SLOT + 2 * pair) * width
                    lanes = pl.ds((i // 2) * LANES, LANES)
                    left = gathered[pl.ds(r0, width), lanes]
                    right = gathered[pl.ds(r0 + width, width), lanes]
                    if i % 2 == 0:
                        joined = jnp.where(low, left, pltpu.roll(right, held, 1))
                    else:
                        joined = jnp.where(low, pltpu.roll(left, held, 1), right)
                    paired[i, pl.ds(c * width, width), pl.ds(pair * LANES, LANES)] = (
                        joined.astype(BF16)
                    )
        ends = (start + live).reshape(nx, held, 1)
        over = [jnp.maximum(ends[i, held - 1 : held] - base, 0) for i in range(nx)]
        pool = None
        for i in range(nx):
            pooled = jnp.zeros((1, 1), jnp.int32)
            for j in range(nx):
                if j != i:
                    ahead_of = lax.rem(x + j, nx) < lax.rem(x + i, nx)
                    pooled += jnp.where(ahead_of, over[j], 0)
            live_i = live[i * held : (i + 1) * held]
            start_i = start[i * held : (i + 1) * held]
            far = lane - (cap + LANES)
            far = jnp.where(far >= pooled, far - pooled + base, -1)
            rank = jnp.where(lane < cap + LANES, jnp.where(lane < base, lane, -1), far)
            slot = rank - start_i
            slot = jnp.where((slot < live_i) & (rank >= 0), slot, -1).astype(F32).astype(BF16)
            for s in range(SLOT):
                chosen[pl.ds(s * held, held), :] = jnp.where(
                    slot == float(s), jnp.ones_like(slot), jnp.zeros_like(slot)
                )
            block = dot(paired[i], chosen[...])
            n = nx * q + i
            send_a[n, :, pl.ds(0, cap)] = block[:width, :cap].astype(BF16)
            send_a[n, :, pl.ds(cap, cap)] = block[width:, :cap].astype(BF16)
            re, im = block[:width, cap : cap + LANES], block[width:, cap : cap + LANES]
            send_b[n] = jnp.where(low, re, pltpu.roll(im, held, 1)).astype(BF16)
            extra = block[:, cap + LANES :]
            pool = extra if pool is None else pool + extra
            if first:
                if i == 1:
                    pl.semaphore_wait(barrier, nx * nz - 1 + nl - 1)
                if i > 0:
                    a_copy(q, i - 1).start()
            elif i == 0:
                a_copy(q - 1, nx - 1).start()
                p_copy(q - 1).start()

                @pl.when(q == last)
                def _():
                    members(start_i, live_i, pooled)

            elif i == 1:

                @pl.when(q < last)
                def _():
                    a_copy(q, 0).start()

                @pl.when(q == last)
                def _():
                    own_a.start()
                    own_b.start()

            else:
                a_copy(q, i - 1).start()
        send_p[q, :, pl.ds(0, LANES)] = pool[:width].astype(BF16)
        send_p[q, :, pl.ds(LANES, LANES)] = pool[width:].astype(BF16)

    column(0, True)

    def later(q, carry):
        column(q, False)
        return carry

    lax.fori_loop(1, nz, later, 0)
    bin_send[...] = jnp.full(bin_send.shape, bin_ref[0], jnp.int32).astype(F32).astype(BF16)
    a_copy(last, nx - 1).start()
    own_p.start()

    def others(each):
        def some(q, carry):
            for i in range(nx):
                if i > 0:
                    each(q, i)
                else:

                    @pl.when(q < last)
                    def _():
                        each(q, 0)

            return carry

        lax.fori_loop(0, nz, some, 0)

    others(lambda q, i: b_copy(q, i).start())

    def bin_copy(dl):
        return pltpu.make_async_remote_copy(
            src_ref=bin_send,
            dst_ref=bin_land.at[lst],
            send_sem=n_send.at[dl],
            recv_sem=n_recv.at[dl],
            device_id=(lax.rem(lst + dl, nl), chan),
            device_id_type=MESH,
        )

    for dl in range(1, nl):
        bin_copy(dl).start()
    bin_land[lst] = bin_send[...]

    steps = step_cos.shape[0]
    bases = half // steps
    unit = 2.0 * math.pi / channels
    shape = (16, channels)
    bit = lax.broadcasted_iota(jnp.int32, shape, 0)
    f = lax.broadcasted_iota(jnp.int32, shape, 1).astype(F32)
    power = jnp.zeros(shape, F32)
    for n in range(10):
        power = jnp.where(bit == n, float(2**n), power)
    product = power * f
    angle = (product - jnp.floor(product * (1.0 / channels)) * channels) * unit
    bit_cos, bit_sin = jnp.cos(angle), jnp.sin(angle)
    shape = (8, channels)
    within = lax.broadcasted_iota(jnp.int32, shape, 0)

    def turned_by(v, n):
        c, s = bit_cos[n : n + 1], bit_sin[n : n + 1]
        return v[0] * c - v[1] * s, v[1] * c + v[0] * s

    def eight(low_bit, v):
        for n in range(3):
            w = turned_by(v, low_bit + n)
            on = (within // 2**n) % 2 == 1
            v = tuple(jnp.where(on, new, old) for new, old in zip(w, v))
        return v

    tiles = [eight(0, (jnp.ones(shape, F32), jnp.zeros(shape, F32)))]
    for n in range(3, 6):
        tiles += [turned_by(v, n) for v in tiles]
    for n, v in enumerate(tiles):
        step_cos[pl.ds(8 * n, 8), :], step_sin[pl.ds(8 * n, 8), :] = v
    f = f[:8] * unit
    taper = (
        0.35875
        - 0.48829 * bit_cos[:1]
        + 0.14128 * bit_cos[1:2]
        - 0.01168 * jnp.cos(3.0 * f)[:1]
    ) * (2.0 / math.sqrt(channels))
    v = eight(6, (jnp.broadcast_to(taper, shape), jnp.zeros(shape, F32)))
    base_cos[pl.ds(0, 8), :], base_sin[pl.ds(0, 8), :] = v
    base_cos[pl.ds(8, 8), :], base_sin[pl.ds(8, 8), :] = turned_by(v, 9)
    channel = lax.broadcasted_iota(jnp.int32, (1, channels), 1)
    middle = taper * jnp.where(channel % 2 == 0, 1.0, -1.0)
    step_row = lax.broadcasted_iota(jnp.int32, (steps, channels), 0)

    def tables(a, carry):
        bc, bs = base_cos[pl.ds(a, 1), :], base_sin[pl.ds(a, 1), :]
        uc, us = step_cos[...], step_sin[...]
        at = pl.multiple_of(a * steps, steps)
        table[pl.ds(at, steps), :] = (uc * bc - us * bs).astype(BF16)
        sines = jnp.where(step_row + at == 0, middle, us * bc + uc * bs)
        table[pl.ds(half + at, steps), :] = sines.astype(BF16)
        return carry

    lax.fori_loop(0, bases, tables, 0)
    cov_copy.wait()
    tall = 256

    def folding(i, carry):
        at = pl.ds(pl.multiple_of(i * tall, tall), tall)
        fold[at, :] = dot(table[at, :], cov[...]).astype(BF16)
        return carry

    folds = channels // tall
    ahead_folds = folds - nz // 2
    lax.fori_loop(0, ahead_folds, folding, 0)

    def pass_on(q):
        for j in range(1, nx):
            f_copy(q, j).start()

    def folding_on(i, carry):
        q = 2 * (i - ahead_folds)
        p_copy(q).wait_recv()
        pass_on(q)

        @pl.when(q + 1 < last)
        def _():
            p_copy(q + 1).wait_recv()

        @pl.when(q + 1 == last)
        def _():
            own_p.wait()

        pass_on(q + 1)
        return folding(i, carry)

    lax.fori_loop(ahead_folds, folds, folding_on, 0)

    def swap(v, w):
        if w < LANES:
            return pltpu.roll(v, w, 1)
        return jnp.concatenate([v[:, w:], v[:, :w]], axis=1)

    def partial(h, rows, member, w):
        at = pl.multiple_of(h * part, part)
        c = dot(fold[pl.ds(at, part), :], rows[...])
        s = dot(fold[pl.ds(half + at, part), :], rows[...])
        first = lax.broadcasted_iota(jnp.int32, (part, 1), 0) + at == 0
        mine = member[...]

        def total(v):
            return dot(v, mine, NT)

        def exact(v):
            top = v.astype(BF16)
            return total(top) + total((v - top.astype(F32)).astype(BF16))

        if w < LANES:
            cr, sr = swap(c, w), swap(s, w)
            even, odd = c * c + cr * cr, s * s + sr * sr
            cross = 2.0 * (c * sr - cr * s)
            lane = lax.broadcasted_iota(jnp.int32, (1, 2 * w), 1)
            powers = jnp.where(first, jnp.where(lane < w, even, odd), even + odd + cross)
        else:
            rc, ic, rs, im = c[:, :w], c[:, w:], s[:, :w], s[:, w:]
            even, odd = rc * rc + ic * ic, rs * rs + im * im
            cross = 2.0 * (rc * im - ic * rs)
            powers = jnp.concatenate(
                [jnp.where(first, even, even + odd + cross), jnp.where(first, odd, even + odd - cross)],
                axis=1,
            )
        return exact(c), exact(s), total(powers.astype(BF16)), first

    own_a.wait()
    others(lambda q, i: a_copy(q, i).wait_recv())

    def part_a(h, carry):
        at = pl.ds(pl.multiple_of(h * part, part), part)
        for n, v in enumerate(partial(h, rows_a, member_a, cap)[:3]):
            sums[n, at, :] = v
        return carry

    lax.fori_loop(0, spans, part_a, 0)

    def forwarded(q, carry):
        for j in range(1, nx):
            f_copy(q, j).wait_recv()
        return carry

    lax.fori_loop(0, nz, forwarded, 0)

    def part_p(h, carry):
        at = pl.ds(pl.multiple_of(h * part, part), part)
        for n, v in enumerate(partial(h, rows_p, member_p, LANES)[:3]):
            sums[n, at, :] += v
        return carry

    lax.fori_loop(0, spans, part_p, 0)
    own_b.wait()
    others(lambda q, i: b_copy(q, i).wait_recv())

    def share_copy(source, h, to, dl):
        return pltpu.make_async_remote_copy(
            src_ref=source.at[h],
            dst_ref=landed.at[lst],
            send_sem=y_send.at[to],
            recv_sem=y_recv.at[dl],
            device_id=(to, chan),
            device_id_type=MESH,
        )

    def share(source, h, to):
        @pl.when(to != lst)
        def _():
            share_copy(source, h, to, lax.rem(to - lst + nl, nl)).start()

        @pl.when(to == lst)
        def _():
            landed[lst] = source[h]

    tall_share = part // 2
    below = lax.broadcasted_iota(jnp.int32, (part, LANES), 1) < held
    for h in range(spans):
        share_plus[h, pl.ds(tall_share, TAIL), :] = jnp.zeros((TAIL, LANES), BF16)

    def finish(h, carry):
        at = pl.ds(pl.multiple_of(h * part, part), part)
        c, s, p, first = partial(h, rows_b, member_b, held)
        c, s, p = c + sums[0, at, :], s + sums[1, at, :], p + sums[2, at, :]
        turned = jnp.where(below, 1.0, -1.0) * pltpu.roll(s, held, 1)
        up = jnp.where(first, c, c + turned)
        down = jnp.where(first, s, c - turned)
        up, down = up * up, down * down
        whole = jnp.where(below, up + pltpu.roll(up, held, 1), down + pltpu.roll(down, held, 1))
        crossed = (whole - p) * scale_ref[:1, :]
        top, bottom = crossed[:tall_share], crossed[tall_share:]
        under = below[:tall_share]
        share_plus[h, pl.ds(0, tall_share), :] = jnp.where(
            under, top, pltpu.roll(bottom, held, 1)
        ).astype(BF16)
        minus = jnp.where(under, pltpu.roll(top, held, 1), bottom).astype(BF16)
        share_minus[h, pl.ds(0, tall_share), :] = minus

        @pl.when(h == 0)
        def _():
            share_minus[spans - 1, pl.ds(tall_share, TAIL), :] = minus[:TAIL]

        @pl.when(h > 0)
        def _():
            share_minus[h - 1, pl.ds(tall_share, TAIL), :] = minus[:TAIL]
            share(share_plus, h - 1, h - 1)

        @pl.when(h > 1)
        def _():
            share(share_minus, h - 2, nl + 1 - h)

        return carry

    lax.fori_loop(0, spans, finish, 0)
    share(share_plus, spans - 1, spans - 1)
    share(share_minus, spans - 2, nl + 1 - spans)
    share(share_minus, spans - 1, nl - spans)

    row = lax.broadcasted_iota(jnp.int32, (tall_share + TAIL, part), 0)
    col = lax.broadcasted_iota(jnp.int32, (tall_share + TAIL, part), 1)
    want = jnp.where(lst < spans, col, part - col)
    lower = one_if((row == want) & (row < tall_share) | (row == want - tall_share) & (want == part))
    upper = one_if((row + tall_share == want) & (row < tall_share))
    turn = jnp.concatenate([lower, upper], axis=1)

    def order(t):
        both = dot(landed[t], turn, TN)
        pieces[t] = both[:held, :part] + both[held:, part:]

    order(lst)
    for dl in range(1, nl):
        bin_copy(dl).wait()
        share_copy(share_plus, 0, lax.rem(lst + dl, nl), dl).wait_recv()
        order(lax.rem(lst + nl - dl, nl))
    codes = [bin_land[t].astype(F32)[:1, :1] for t in range(nl)]
    for b in range(NBIN):
        total = jnp.zeros((held, part), F32)
        count = jnp.zeros((1, 1), F32)
        for t in range(nl):
            inside = codes[t] == b
            total += jnp.where(inside, pieces[t], 0.0)
            count += jnp.where(inside, 1.0, 0.0)
        out_ref[b] = total * (1.0 / jnp.maximum(count, 1.0))

    others(lambda q, i: a_copy(q, i).wait_send())
    others(lambda q, i: b_copy(q, i).wait_send())

    def sent(q, carry):
        for j in range(1, nx):
            f_copy(q, j).wait_send()

        @pl.when(q < last)
        def _():
            p_copy(q).wait_send()

        return carry

    lax.fori_loop(0, nz, sent, 0)
    for dl in range(1, nl):
        share_copy(share_plus, 0, lax.rem(lst + dl, nl), dl).wait_send()


def cross_power(cap, collective_id, sizes, lst_bin, owner, size, vis, cov):
    nx, nz, nl, held, channels, width = sizes
    half = channels // 2
    part = channels // nl
    total = nx * nz
    vmem = pltpu.VMEM
    dma = pltpu.SemaphoreType.DMA
    share = (channels // (2 * part), part // 2 + TAIL, LANES)
    return pl.pallas_call(
        functools.partial(kernel, cap, sizes),
        out_shape=jax.ShapeDtypeStruct((NBIN, held, part), F32),
        in_specs=[
            pl.BlockSpec(memory_space=pltpu.SMEM),
            pl.BlockSpec(memory_space=vmem),
            pl.BlockSpec(memory_space=vmem),
            pl.BlockSpec(memory_space=vmem),
            pl.BlockSpec(memory_space=pl.ANY),
        ],
        out_specs=pl.BlockSpec(memory_space=vmem),
        scratch_shapes=[
            vmem((channels, channels), BF16),
            vmem((nx * held, owner.shape[1]), BF16),
            vmem((SLOT * held, cap + 2 * LANES), BF16),
            vmem((2 * SLOT * width, nx * held), F32),
            vmem((nx, 2 * width, SLOT * held), BF16),
            vmem((total, width, 2 * cap), BF16),
            vmem((total, width, LANES), BF16),
            vmem((nz, width, 2 * LANES), BF16),
            vmem((channels, 2 * cap), BF16),
            vmem((channels, LANES), BF16),
            vmem((channels, 2 * LANES), BF16),
            vmem((channels, channels), BF16),
            vmem((channels, channels), BF16),
            vmem((64, channels), F32),
            vmem((64, channels), F32),
            vmem((16, channels), F32),
            vmem((16, channels), F32),
            vmem((2 * held, 2 * cap), BF16),
            vmem((2 * held, LANES), BF16),
            vmem((2 * held, 2 * LANES), BF16),
            vmem((8, LANES), F32),
            vmem((3, half, LANES), F32),
            vmem(share, BF16),
            vmem(share, BF16),
            vmem((nl,) + share[1:], BF16),
            vmem((nl, held, part), F32),
            vmem((16, LANES), BF16),
            vmem((nl, 16, LANES), BF16),
            dma(()),
            dma((3,)),
            dma((total,)),
            dma((total,)),
            dma((total,)),
            dma((total,)),
            dma((nz,)),
            dma((nz,)),
            dma((nz * (nx - 1),)),
            dma((nz * (nx - 1),)),
            dma((nl,)),
            dma((nl,)),
            dma((nl,)),
            dma((nl,)),
        ],
        compiler_params=pltpu.CompilerParams(
            collective_id=collective_id, has_side_effects=True, vmem_limit_bytes=60 * 2**20
        ),
    )(lst_bin, owner, size, vis, cov)


def solution(mesh):
    nl, total = mesh.shape["lst"], mesh.shape["chan"]
    nx = total // 8
    nz = total // nx

    def shards(visibility, inverse_cov, group_size, group_owner, lst_bin):
        groups, width = visibility.shape[2], visibility.shape[4]
        channels = inverse_cov.shape[0]
        held = groups // total
        sizes = (nx, nz, nl, held, channels, width)
        vis = jnp.transpose(visibility, (0, 1, 3, 4, 2)).reshape(2 * SLOT * width, groups)
        owner = group_owner.reshape(1, groups)
        size = group_size.reshape(1, groups)
        full = SLOT * held
        tight = full // 2
        fits = pl.pallas_call(
            functools.partial(fits_kernel, tight + held, LANES, sizes),
            out_shape=jax.ShapeDtypeStruct((1,), jnp.int32),
            out_specs=pl.BlockSpec(memory_space=pltpu.SMEM),
        )(owner, size)
        return lax.cond(
            fits[0] > 0,
            functools.partial(cross_power, tight, 0, sizes),
            functools.partial(cross_power, full, 1, sizes),
            lst_bin, owner, size, vis, inverse_cov,
        )

    placed = (P(None, "lst", None, None, "chan"), P(), P(), P(), P("lst"))
    return jax.shard_map(
        shards, mesh=mesh, in_specs=placed, out_specs=P(None, "chan", "lst"), check_vma=False
    )
```

```python
import functools
import math

import jax
import jax.numpy as jnp
from jax import lax
from jax.experimental import pallas as pl
from jax.experimental.pallas import tpu as pltpu
from jax.sharding import PartitionSpec as P

NBIN = 8
SLOT = 8
MESH = pl.DeviceIdType.MESH
F32 = jnp.float32
BF16 = jnp.bfloat16
NN = (((1,), (0,)), ((), ()))
NT = (((1,), (1,)), ((), ()))
TN = (((0,), (0,)), ((), ()))
TAIL = 16
LANES = 128


def dot(a, b, dims=NN):
    return lax.dot_general(a, b, dims, preferred_element_type=F32)


def one_if(condition):
    return jnp.where(condition, 1.0, 0.0).astype(BF16)


def fits_kernel(base, room, sizes, owner_ref, size_ref, out_ref):
    nx, nz, nl, held, channels, width = sizes
    first = lax.broadcasted_iota(jnp.int32, (nx * nz, 1), 0) * held
    owner = owner_ref[...]
    mine = (owner >= first) & (owner < first + held)
    lives = jnp.sum(jnp.where(mine, size_ref[...], 0), axis=1, keepdims=True)
    over = jnp.maximum(lives - base, 0).reshape(nx, nz, 1)
    out_ref[0] = jnp.where(jnp.max(jnp.sum(over, axis=0)) <= room, 1, 0)


def kernel(
    cap,
    sizes,
    bin_ref,
    owner_ref,
    size_ref,
    vis_hbm,
    cov_hbm,
    out_ref,
    vis,
    vis_sem,
    cov,
    pick,
    chosen,
    gathered,
    paired,
    send_a,
    send_b,
    send_p,
    rows_a,
    rows_b,
    rows_p,
    table,
    fold,
    step_cos,
    step_sin,
    base_cos,
    base_sin,
    member_a,
    member_b,
    member_p,
    scale_ref,
    held_ref,
    sums,
    acc_b,
    share_plus,
    share_minus,
    landed,
    pieces,
    bin_send,
    bin_land,
    cov_sem,
    own_sem,
    a_send,
    a_recv,
    b_send,
    b_recv,
    p_send,
    p_recv,
    f_send,
    f_recv,
    y_send,
    y_recv,
    n_send,
    n_recv,
):
    nx, nz, nl, held, channels, width = sizes
    half = channels // 2
    part = channels // nl
    spans = half // part
    base = cap + held
    wide = cap + 2 * LANES
    lst = lax.axis_index("lst")
    chan = lax.axis_index("chan")
    x, z = chan // nz, chan % nz
    last = nz - 1

    def ahead(q):
        return nz // 2 + (1 - 2 * (q % 2)) * ((q + 1) // 2)

    def place(q, i):
        return lax.rem(x + i, nx) * nz + lax.rem(z + ahead(q), nz)

    def rows_of(ref, source):
        return ref.at[pl.ds(pl.multiple_of(source * width, 16), width), :]

    def a_copy(q, i):
        n = nx * q + i
        return pltpu.make_async_remote_copy(
            src_ref=send_a.at[n],
            dst_ref=rows_of(rows_a, chan),
            send_sem=a_send,
            recv_sem=a_recv,
            device_id=(lst, place(q, i)),
            device_id_type=MESH,
        )

    def b_copy(q, i):
        n = nx * q + i
        return pltpu.make_async_remote_copy(
            src_ref=send_b.at[n],
            dst_ref=rows_of(rows_b, chan),
            send_sem=b_send,
            recv_sem=b_recv.at[i],
            device_id=(lst, place(q, i)),
            device_id_type=MESH,
        )

    def p_copy(q):
        return pltpu.make_async_remote_copy(
            src_ref=send_p.at[q],
            dst_ref=rows_of(rows_p, chan),
            send_sem=p_send,
            recv_sem=p_recv.at[q],
            device_id=(lst, place(q, 0)),
            device_id_type=MESH,
        )

    def f_copy(q, j):
        source = x * nz + lax.rem(z + nz - ahead(q), nz)
        return pltpu.make_async_remote_copy(
            src_ref=rows_of(rows_p, source),
            dst_ref=rows_of(rows_p, source),
            send_sem=f_send,
            recv_sem=f_recv,
            device_id=(lst, lax.rem(x + j, nx) * nz + z),
            device_id_type=MESH,
        )

    own_a = pltpu.make_async_copy(send_a.at[nx * last], rows_of(rows_a, chan), own_sem.at[0])
    own_b = pltpu.make_async_copy(send_b.at[nx * last], rows_of(rows_b, chan), own_sem.at[1])
    own_p = pltpu.make_async_copy(send_p.at[last], rows_of(rows_p, chan), own_sem.at[2])
    cov_copy = pltpu.make_async_copy(cov_hbm, cov, cov_sem)

    vis_copy = pltpu.make_async_copy(vis_hbm, vis, vis_sem)
    vis_copy.start()
    barrier = pltpu.get_barrier_semaphore()
    for other in range(1, nx * nz):
        peer = lax.rem(x + other // nz, nx) * nz + lax.rem(z + other % nz, nz)
        pl.semaphore_signal(barrier, inc=1, device_id=(lst, peer), device_id_type=MESH)
    for dl in range(1, nl):
        pl.semaphore_signal(
            barrier, inc=1, device_id=(lax.rem(lst + dl, nl), chan), device_id_type=MESH
        )

    low = lax.broadcasted_iota(jnp.int32, (width, LANES), 1) < held
    lane = lax.broadcasted_iota(jnp.int32, (1, wide), 1)
    spot = lax.broadcasted_iota(jnp.int32, (held, LANES), 0).astype(F32).astype(BF16)
    row_id = lax.broadcasted_iota(jnp.int32, (nx * held, nx * held), 0)
    col_id = lax.broadcasted_iota(jnp.int32, (nx * held, nx * held), 1)
    before = one_if((row_id // held == col_id // held) & (col_id < row_id))
    one, none = jnp.ones((held, LANES), BF16), jnp.zeros((held, LANES), BF16)

    def members(start, live, pooled):
        at = lax.broadcasted_iota(jnp.int32, (held, cap), 1)
        mine = one_if((at >= start) & (at < start + live))
        empty = jnp.zeros((held, cap), BF16)
        member_a[pl.ds(0, held), :] = jnp.concatenate([mine, empty], axis=1)
        member_a[pl.ds(held, held), :] = jnp.concatenate([empty, mine], axis=1)
        at = lax.broadcasted_iota(jnp.int32, (held, LANES), 1)
        below = at < held
        near = lax.rem(at, held) + cap
        mine = (near >= start) & (near < start + live)
        member_b[pl.ds(0, held), :] = one_if(mine & below)
        member_b[pl.ds(held, held), :] = one_if(mine & jnp.logical_not(below))
        far = at + base - pooled
        mine = one_if((far >= jnp.maximum(start, base)) & (far < start + live))
        empty = jnp.zeros((held, LANES), BF16)
        member_p[pl.ds(0, held), :] = jnp.concatenate([mine, empty], axis=1)
        member_p[pl.ds(held, held), :] = jnp.concatenate([empty, mine], axis=1)
        row_id = lax.broadcasted_iota(jnp.int32, (held, LANES), 0)
        lane = lax.rem(lax.broadcasted_iota(jnp.int32, (held, LANES), 1), held)
        spread = jnp.where(row_id == lane, jnp.broadcast_to(live, (held, LANES)), 0)
        count = jnp.sum(spread.astype(F32), axis=0, keepdims=True)
        scale_ref[...] = jnp.broadcast_to(1.0 / (count * (count - 1.0)), scale_ref.shape)

    def column(q, first):
        groups = owner_ref.shape[1]
        lives = []
        for i in range(nx):
            seat = owner_ref[...] - place(q, i) * held
            seat = jnp.where((seat >= 0) & (seat < held), seat, -1).astype(F32).astype(BF16)
            sized = size_ref[...].astype(F32).astype(BF16)
            live_sum = none
            for g in range(0, groups, LANES):
                hit = jnp.broadcast_to(seat[:, g : g + LANES], (held, LANES)) == spot
                pick[pl.ds(i * held, held), pl.ds(g, LANES)] = jnp.where(hit, one, none)
                sizes_here = jnp.broadcast_to(sized[:, g : g + LANES], (held, LANES))
                live_sum += jnp.where(hit, sizes_here, none)
            lives.append(jnp.sum(live_sum.astype(F32), axis=1, keepdims=True))
        live = jnp.concatenate(lives, axis=0)
        if not first:
            for i in range(nx - 1):

                @pl.when(q > 1)
                def _():
                    a_copy(q - 1, i).start()

            a_copy(q - 1, nx - 1).start()
            p_copy(q - 1).start()
        live_wide = jnp.broadcast_to(live, (nx * held, LANES)).astype(BF16)
        start = dot(before, live_wide)[:, :1].astype(jnp.int32)
        live = live.astype(jnp.int32)
        if first:
            vis_copy.wait()
            cov_copy.start()
        gathered[...] = dot(vis[...], pick[...], NT)
        for i in range(nx):
            for c in range(2):
                for pair in range(SLOT // 2):
                    r0 = (c * SLOT + 2 * pair) * width
                    lanes = pl.ds((i // 2) * LANES, LANES)
                    left = gathered[pl.ds(r0, width), lanes]
                    right = gathered[pl.ds(r0 + width, width), lanes]
                    if i % 2 == 0:
                        joined = jnp.where(low, left, pltpu.roll(right, held, 1))
                    else:
                        joined = jnp.where(low, pltpu.roll(left, held, 1), right)
                    paired[i, pl.ds(c * width, width), pl.ds(pair * LANES, LANES)] = (
                        joined.astype(BF16)
                    )
        ends = (start + live).reshape(nx, held, 1)
        over = [jnp.maximum(ends[i, held - 1 : held] - base, 0) for i in range(nx)]
        pool = None
        for i in range(nx):
            pooled = jnp.zeros((1, 1), jnp.int32)
            for j in range(nx):
                if j != i:
                    ahead_of = lax.rem(x + j, nx) < lax.rem(x + i, nx)
                    pooled += jnp.where(ahead_of, over[j], 0)
            live_i = live[i * held : (i + 1) * held]
            start_i = start[i * held : (i + 1) * held]
            far = lane - (cap + LANES)
            far = jnp.where(far >= pooled, far - pooled + base, -1)
            rank = jnp.where(lane < cap + LANES, jnp.where(lane < base, lane, -1), far)
            slot = rank - start_i
            slot = jnp.where((slot < live_i) & (rank >= 0), slot, -1).astype(F32).astype(BF16)
            for s in range(SLOT):
                chosen[i, pl.ds(s * held, held), :] = jnp.where(
                    slot == float(s), jnp.ones_like(slot), jnp.zeros_like(slot)
                )
            block = dot(paired[i], chosen[i])
            if i == 0:
                held_ref[0] = jnp.broadcast_to(live_i, (held, LANES))
                held_ref[1] = jnp.broadcast_to(start_i, (held, LANES))
                held_ref[2] = jnp.broadcast_to(pooled, (held, LANES))
            n = nx * q + i
            send_a[n, :, pl.ds(0, cap)] = block[:width, :cap].astype(BF16)
            send_a[n, :, pl.ds(cap, cap)] = block[width:, :cap].astype(BF16)
            re, im = block[:width, cap : cap + LANES], block[width:, cap : cap + LANES]
            send_b[n] = jnp.where(low, re, pltpu.roll(im, held, 1)).astype(BF16)
            extra = block[:, cap + LANES :]
            pool = extra if pool is None else pool + extra
        send_p[q, :, pl.ds(0, LANES)] = pool[:width].astype(BF16)
        send_p[q, :, pl.ds(LANES, LANES)] = pool[width:].astype(BF16)

    column(0, True)
    pl.semaphore_wait(barrier, nx * nz - 1 + nl - 1)
    for i in range(nx - 1):
        a_copy(0, i).start()

    def later(q, carry):
        column(q, False)
        return carry

    lax.fori_loop(1, nz, later, 0)
    bin_send[...] = jnp.full(bin_send.shape, bin_ref[0], jnp.int32).astype(F32).astype(BF16)
    for i in range(1, nx):
        a_copy(last, i).start()
    own_a.start()
    own_b.start()
    own_p.start()

    def await_all(like, semaphore):
        pltpu.make_async_copy(like, like, semaphore).wait()

    blocks = nx * nz - 1
    for i in (1, 2, 3, 0):

        def start_b(q, carry):
            b_copy(q, i).start()
            return carry

        lax.fori_loop(0, nz - (i == 0), start_b, 0)
    members(held_ref[1][:, :1], held_ref[0][:, :1], held_ref[2][:1, :1])

    def bin_copy(dl):
        return pltpu.make_async_remote_copy(
            src_ref=bin_send,
            dst_ref=bin_land.at[lst],
            send_sem=n_send,
            recv_sem=n_recv,
            device_id=(lax.rem(lst + dl, nl), chan),
            device_id_type=MESH,
        )

    for dl in range(1, nl):
        bin_copy(dl).start()
    bin_land[lst] = bin_send[...]

    steps = step_cos.shape[0]
    bases = half // steps
    unit = 2.0 * math.pi / channels
    shape = (16, channels)
    bit = lax.broadcasted_iota(jnp.int32, shape, 0)
    f = lax.broadcasted_iota(jnp.int32, shape, 1).astype(F32)
    power = jnp.zeros(shape, F32)
    for n in range(10):
        power = jnp.where(bit == n, float(2**n), power)
    product = power * f
    angle = (product - jnp.floor(product * (1.0 / channels)) * channels) * unit
    bit_cos, bit_sin = jnp.cos(angle), jnp.sin(angle)
    shape = (8, channels)
    within = lax.broadcasted_iota(jnp.int32, shape, 0)

    def turned_by(v, n):
        c, s = bit_cos[n : n + 1], bit_sin[n : n + 1]
        return v[0] * c - v[1] * s, v[1] * c + v[0] * s

    def eight(low_bit, v):
        for n in range(3):
            w = turned_by(v, low_bit + n)
            on = (within // 2**n) % 2 == 1
            v = tuple(jnp.where(on, new, old) for new, old in zip(w, v))
        return v

    tiles = [eight(0, (jnp.ones(shape, F32), jnp.zeros(shape, F32)))]
    for n in range(3, 6):
        tiles += [turned_by(v, n) for v in tiles]
    for n, v in enumerate(tiles):
        step_cos[pl.ds(8 * n, 8), :], step_sin[pl.ds(8 * n, 8), :] = v
    f = f[:8] * unit
    taper = (
        0.35875
        - 0.48829 * bit_cos[:1]
        + 0.14128 * bit_cos[1:2]
        - 0.01168 * jnp.cos(3.0 * f)[:1]
    ) * (2.0 / math.sqrt(channels))
    v = eight(6, (jnp.broadcast_to(taper, shape), jnp.zeros(shape, F32)))
    base_cos[pl.ds(0, 8), :], base_sin[pl.ds(0, 8), :] = v
    base_cos[pl.ds(8, 8), :], base_sin[pl.ds(8, 8), :] = turned_by(v, 9)
    channel = lax.broadcasted_iota(jnp.int32, (1, channels), 1)
    middle = taper * jnp.where(channel % 2 == 0, 1.0, -1.0)
    step_row = lax.broadcasted_iota(jnp.int32, (steps, channels), 0)

    def tables(a, carry):
        bc, bs = base_cos[pl.ds(a, 1), :], base_sin[pl.ds(a, 1), :]
        uc, us = step_cos[...], step_sin[...]
        at = pl.multiple_of(a * steps, steps)
        table[pl.ds(at, steps), :] = (uc * bc - us * bs).astype(BF16)
        sines = jnp.where(step_row + at == 0, middle, us * bc + uc * bs)
        table[pl.ds(half + at, steps), :] = sines.astype(BF16)
        return carry

    lax.fori_loop(0, bases, tables, 0)
    cov_copy.wait()
    tall = 256

    def folding(i, carry):
        at = pl.ds(pl.multiple_of(i * tall, tall), tall)
        fold[at, :] = dot(table[at, :], cov[...]).astype(BF16)
        return carry

    folds = channels // tall
    ahead_folds = folds - nz // 2
    lax.fori_loop(0, ahead_folds, folding, 0)

    def pass_on(q):
        for j in range(1, nx):
            f_copy(q, j).start()

    def folding_on(i, carry):
        q = 2 * (i - ahead_folds)
        p_copy(q).wait_recv()
        pass_on(q)

        @pl.when(q + 1 < last)
        def _():
            p_copy(q + 1).wait_recv()

        @pl.when(q + 1 == last)
        def _():
            own_p.wait()

        pass_on(q + 1)
        return folding(i, carry)

    lax.fori_loop(ahead_folds, folds, folding_on, 0)

    def swap(v, w):
        if w < LANES:
            return pltpu.roll(v, w, 1)
        return jnp.concatenate([v[:, w:], v[:, :w]], axis=1)

    def partial(h, rows, member, w):
        at = h * part if isinstance(h, int) else pl.multiple_of(h * part, part)
        if rows is None:
            c = acc_b[pl.ds(at, part), :]
            s = acc_b[pl.ds(half + at, part), :]
        else:
            c = dot(fold[pl.ds(at, part), :], rows[...])
            s = dot(fold[pl.ds(half + at, part), :], rows[...])
        first = lax.broadcasted_iota(jnp.int32, (part, 1), 0) + at == 0
        mine = member[...]

        def total(v):
            return dot(v, mine, NT)

        def exact(v):
            top = v.astype(BF16)
            return total(top) + total((v - top.astype(F32)).astype(BF16))

        if w < LANES:
            cr, sr = swap(c, w), swap(s, w)
            even, odd = c * c + cr * cr, s * s + sr * sr
            cross = 2.0 * (c * sr - cr * s)
            lane = lax.broadcasted_iota(jnp.int32, (1, 2 * w), 1)
            powers = jnp.where(first, jnp.where(lane < w, even, odd), even + odd + cross)
        else:
            rc, ic, rs, im = c[:, :w], c[:, w:], s[:, :w], s[:, w:]
            even, odd = rc * rc + ic * ic, rs * rs + im * im
            cross = 2.0 * (rc * im - ic * rs)
            powers = jnp.concatenate(
                [jnp.where(first, even, even + odd + cross), jnp.where(first, odd, even + odd - cross)],
                axis=1,
            )
        return exact(c), exact(s), total(powers.astype(BF16)), first

    own_a.wait()
    await_all(send_a.at[pl.ds(0, blocks)], a_recv)

    def part_a(h, carry):
        at = pl.ds(pl.multiple_of(h * part, part), part)
        for n, v in enumerate(partial(h, rows_a, member_a, cap)[:3]):
            sums[n, at, :] = v
        return carry

    lax.fori_loop(0, spans, part_a, 0)

    relayed = rows_p.at[pl.ds(0, nz * (nx - 1) * width), :]
    await_all(relayed, f_recv)

    def part_p(h, carry):
        at = pl.ds(pl.multiple_of(h * part, part), part)
        for n, v in enumerate(partial(h, rows_p, member_p, LANES)[:3]):
            sums[n, at, :] += v
        return carry

    lax.fori_loop(0, spans, part_p, 0)
    await_all(send_a.at[pl.ds(0, blocks)], a_send)
    await_all(send_p.at[pl.ds(0, last)], p_send)
    await_all(relayed, f_send)
    await_all(bin_land.at[pl.ds(0, nl - 1)], n_send)
    await_all(bin_land.at[pl.ds(0, nl - 1)], n_recv)
    deep = nz * width
    for i in (1, 2, 3, 0):
        await_all(send_b.at[pl.ds(0, nz - (i == 0))], b_recv.at[i])
        if i == 0:
            own_b.wait()
        ch = pl.ds(pl.multiple_of(lax.rem(x + nx - i, nx) * deep, deep), deep)
        term = dot(fold[:, ch], rows_b[ch, :])
        if i == 1:
            acc_b[...] = term
        else:
            acc_b[...] += term

    def share_copy(source, h, to):
        return pltpu.make_async_remote_copy(
            src_ref=source.at[h],
            dst_ref=landed.at[lst],
            send_sem=y_send,
            recv_sem=y_recv,
            device_id=(to, chan),
            device_id_type=MESH,
        )

    def share(source, h, to):
        @pl.when(to != lst)
        def _():
            share_copy(source, h, to).start()

        @pl.when(to == lst)
        def _():
            landed[lst] = source[h]

    tall_share = part // 2
    below = lax.broadcasted_iota(jnp.int32, (part, LANES), 1) < held
    for h in range(spans):
        share_plus[h, pl.ds(tall_share, TAIL), :] = jnp.zeros((TAIL, LANES), BF16)

    def finish(h):
        at = pl.ds(h * part, part)
        c, s, p, first = partial(h, None, member_b, held)
        c, s, p = c + sums[0, at, :], s + sums[1, at, :], p + sums[2, at, :]
        turned = jnp.where(below, 1.0, -1.0) * pltpu.roll(s, held, 1)
        up = jnp.where(first, c, c + turned)
        down = jnp.where(first, s, c - turned)
        up, down = up * up, down * down
        whole = jnp.where(below, up + pltpu.roll(up, held, 1), down + pltpu.roll(down, held, 1))
        crossed = (whole - p) * scale_ref[:1, :]
        top, bottom = crossed[:tall_share], crossed[tall_share:]
        under = below[:tall_share]
        share_plus[h, pl.ds(0, tall_share), :] = jnp.where(
            under, top, pltpu.roll(bottom, held, 1)
        ).astype(BF16)
        minus = jnp.where(under, pltpu.roll(top, held, 1), bottom).astype(BF16)
        share_minus[h, pl.ds(0, tall_share), :] = minus

        share_minus[(h - 1) % spans, pl.ds(tall_share, TAIL), :] = minus[:TAIL]

    for h in range(spans):
        if h == 2:
            share(share_plus, 0, 0)
            share(share_plus, 1, 1)
            share(share_minus, 0, nl - 1)
        finish(h)
    for h in range(2, spans):
        share(share_plus, h, h)
    for h in range(1, spans):
        share(share_minus, h, nl - 1 - h)

    row = lax.broadcasted_iota(jnp.int32, (tall_share + TAIL, part), 0)
    col = lax.broadcasted_iota(jnp.int32, (tall_share + TAIL, part), 1)
    want = jnp.where(lst < spans, col, part - col)
    lower = one_if((row == want) & (row < tall_share) | (row == want - tall_share) & (want == part))
    upper = one_if((row + tall_share == want) & (row < tall_share))
    turn = jnp.concatenate([lower, upper], axis=1)

    def order(t):
        both = dot(landed[t], turn, TN)
        pieces[t] = both[:held, :part] + both[held:, part:]

    await_all(send_b.at[pl.ds(0, blocks)], b_send)
    order(lst)
    await_all(landed.at[pl.ds(0, nl - 1)], y_recv)
    for dl in range(1, nl):
        order(lax.rem(lst + dl, nl))
    codes = [bin_land[t].astype(F32)[:1, :1] for t in range(nl)]
    for b in range(NBIN):
        total = jnp.zeros((held, part), F32)
        count = jnp.zeros((1, 1), F32)
        for t in range(nl):
            inside = codes[t] == b
            total += jnp.where(inside, pieces[t], 0.0)
            count += jnp.where(inside, 1.0, 0.0)
        out_ref[b] = total * (1.0 / jnp.maximum(count, 1.0))

    await_all(landed.at[pl.ds(0, nl - 1)], y_send)


def cross_power(cap, collective_id, sizes, lst_bin, owner, size, vis, cov):
    nx, nz, nl, held, channels, width = sizes
    half = channels // 2
    part = channels // nl
    total = nx * nz
    vmem = pltpu.VMEM
    dma = pltpu.SemaphoreType.DMA
    share = (channels // (2 * part), part // 2 + TAIL, LANES)
    return pl.pallas_call(
        functools.partial(kernel, cap, sizes),
        out_shape=jax.ShapeDtypeStruct((NBIN, held, part), F32),
        in_specs=[
            pl.BlockSpec(memory_space=pltpu.SMEM),
            pl.BlockSpec(memory_space=vmem),
            pl.BlockSpec(memory_space=vmem),
            pl.BlockSpec(memory_space=pl.ANY),
            pl.BlockSpec(memory_space=pl.ANY),
        ],
        out_specs=pl.BlockSpec(memory_space=vmem),
        scratch_shapes=[
            vmem(vis.shape, BF16),
            dma(()),
            vmem((channels, channels), BF16),
            vmem((nx * held, owner.shape[1]), BF16),
            vmem((nx, SLOT * held, cap + 2 * LANES), BF16),
            vmem((2 * SLOT * width, nx * held), F32),
            vmem((nx, 2 * width, SLOT * held), BF16),
            vmem((total, width, 2 * cap), BF16),
            vmem((total, width, LANES), BF16),
            vmem((nz, width, 2 * LANES), BF16),
            vmem((channels, 2 * cap), BF16),
            vmem((channels, LANES), BF16),
            vmem((channels, 2 * LANES), BF16),
            vmem((channels, channels), BF16),
            vmem((channels, channels), BF16),
            vmem((64, channels), F32),
            vmem((64, channels), F32),
            vmem((16, channels), F32),
            vmem((16, channels), F32),
            vmem((2 * held, 2 * cap), BF16),
            vmem((2 * held, LANES), BF16),
            vmem((2 * held, 2 * LANES), BF16),
            vmem((8, LANES), F32),
            vmem((3, held, LANES), jnp.int32),
            vmem((3, half, LANES), F32),
            vmem((channels, LANES), F32),
            vmem(share, BF16),
            vmem(share, BF16),
            vmem((nl,) + share[1:], BF16),
            vmem((nl, held, part), F32),
            vmem((16, LANES), BF16),
            vmem((nl, 16, LANES), BF16),
            dma(()),
            dma((3,)),
            dma(()),
            dma(()),
            dma(()),
            dma((nx,)),
            dma(()),
            dma((nz,)),
            dma(()),
            dma(()),
            dma(()),
            dma(()),
            dma(()),
            dma(()),
        ],
        compiler_params=pltpu.CompilerParams(
            collective_id=collective_id, has_side_effects=True, vmem_limit_bytes=60 * 2**20
        ),
    )(lst_bin, owner, size, vis, cov)


def solution(mesh):
    nl, total = mesh.shape["lst"], mesh.shape["chan"]
    nx = total // 8
    nz = total // nx

    def shards(visibility, inverse_cov, group_size, group_owner, lst_bin):
        groups, width = visibility.shape[2], visibility.shape[4]
        channels = inverse_cov.shape[0]
        held = groups // total
        sizes = (nx, nz, nl, held, channels, width)
        vis = jnp.transpose(visibility, (0, 1, 3, 4, 2)).reshape(2 * SLOT * width, groups)
        owner = group_owner.reshape(1, groups)
        size = group_size.reshape(1, groups)
        full = SLOT * held
        tight = full // 2
        fits = pl.pallas_call(
            functools.partial(fits_kernel, tight + held, LANES, sizes),
            out_shape=jax.ShapeDtypeStruct((1,), jnp.int32),
            out_specs=pl.BlockSpec(memory_space=pltpu.SMEM),
        )(owner, size)
        return lax.cond(
            fits[0] > 0,
            functools.partial(cross_power, tight, 0, sizes),
            functools.partial(cross_power, full, 1, sizes),
            lst_bin, owner, size, vis, inverse_cov,
        )

    placed = (P(None, "lst", None, None, "chan"), P(), P(), P(), P("lst"))
    return jax.shard_map(
        shards, mesh=mesh, in_specs=placed, out_specs=P(None, "chan", "lst"), check_vma=False
    )
```

```python
import functools
import math

import jax
import jax.numpy as jnp
from jax import lax
from jax.experimental import pallas as pl
from jax.experimental.pallas import tpu as pltpu
from jax.sharding import PartitionSpec as P

NBIN = 8
SLOT = 8
MESH = pl.DeviceIdType.MESH
F32 = jnp.float32
BF16 = jnp.bfloat16
NN = (((1,), (0,)), ((), ()))
NT = (((1,), (1,)), ((), ()))
TN = (((0,), (0,)), ((), ()))
TAIL = 16
LANES = 128


def dot(a, b, dims=NN):
    return lax.dot_general(a, b, dims, preferred_element_type=F32)


def one_if(condition):
    return jnp.where(condition, 1.0, 0.0).astype(BF16)


def fits_kernel(base, room, sizes, owner_ref, size_ref, out_ref):
    nx, nz, nl, held, channels, width = sizes
    first = lax.broadcasted_iota(jnp.int32, (nx * nz, 1), 0) * held
    owner = owner_ref[...]
    mine = (owner >= first) & (owner < first + held)
    lives = jnp.sum(jnp.where(mine, size_ref[...], 0), axis=1, keepdims=True)
    over = jnp.maximum(lives - base, 0).reshape(nx, nz, 1)
    out_ref[0] = jnp.where(jnp.max(jnp.sum(over, axis=0)) <= room, 1, 0)


def kernel(
    cap,
    sizes,
    bin_ref,
    owner_ref,
    size_ref,
    vis_hbm,
    cov_hbm,
    out_ref,
    vis,
    vis_sem,
    cov,
    pick,
    chosen,
    gathered,
    paired,
    send_h,
    send_a,
    send_b,
    send_p,
    rows_h,
    rows_a,
    rows_b,
    rows_p,
    table,
    fold,
    step_cos,
    step_sin,
    base_cos,
    base_sin,
    member_h,
    member_a,
    member_b,
    member_p,
    scale_ref,
    held_ref,
    sums,
    acc_b,
    share_plus,
    share_minus,
    landed,
    pieces,
    bin_send,
    bin_land,
    cov_sem,
    own_sem,
    h_send,
    h_recv,
    a_send,
    a_recv,
    b_send,
    b_recv,
    p_send,
    p_recv,
    f_send,
    f_recv,
    y_send,
    y_recv,
    n_send,
    n_recv,
):
    nx, nz, nl, held, channels, width = sizes
    half = channels // 2
    part = channels // nl
    spans = half // part
    base = cap + held
    wide = cap + 2 * LANES
    rest = cap - LANES
    lst = lax.axis_index("lst")
    chan = lax.axis_index("chan")
    x, z = chan // nz, chan % nz
    last = nz - 1

    def ahead(q):
        return nz // 2 + (1 - 2 * (q % 2)) * ((q + 1) // 2)

    def place(q, i):
        return lax.rem(x + i, nx) * nz + lax.rem(z + ahead(q), nz)

    def rows_of(ref, source):
        return ref.at[pl.ds(pl.multiple_of(source * width, 16), width), :]

    def h_copy(q, i):
        n = nx * q + i
        return pltpu.make_async_remote_copy(
            src_ref=send_h.at[n],
            dst_ref=rows_of(rows_h, chan),
            send_sem=h_send,
            recv_sem=h_recv,
            device_id=(lst, place(q, i)),
            device_id_type=MESH,
        )

    def a_copy(q, i):
        n = nx * q + i
        return pltpu.make_async_remote_copy(
            src_ref=send_a.at[n],
            dst_ref=rows_of(rows_a, chan),
            send_sem=a_send,
            recv_sem=a_recv,
            device_id=(lst, place(q, i)),
            device_id_type=MESH,
        )

    def b_copy(q, i):
        n = nx * q + i
        return pltpu.make_async_remote_copy(
            src_ref=send_b.at[n],
            dst_ref=rows_of(rows_b, chan),
            send_sem=b_send,
            recv_sem=b_recv.at[i],
            device_id=(lst, place(q, i)),
            device_id_type=MESH,
        )

    def p_copy(q):
        return pltpu.make_async_remote_copy(
            src_ref=send_p.at[q],
            dst_ref=rows_of(rows_p, chan),
            send_sem=p_send,
            recv_sem=p_recv.at[q],
            device_id=(lst, place(q, 0)),
            device_id_type=MESH,
        )

    def f_copy(q, j):
        source = x * nz + lax.rem(z + nz - ahead(q), nz)
        return pltpu.make_async_remote_copy(
            src_ref=rows_of(rows_p, source),
            dst_ref=rows_of(rows_p, source),
            send_sem=f_send,
            recv_sem=f_recv,
            device_id=(lst, lax.rem(x + j, nx) * nz + z),
            device_id_type=MESH,
        )

    own_h = pltpu.make_async_copy(send_h.at[nx * last], rows_of(rows_h, chan), own_sem.at[3])
    own_a = pltpu.make_async_copy(send_a.at[nx * last], rows_of(rows_a, chan), own_sem.at[0])
    own_b = pltpu.make_async_copy(send_b.at[nx * last], rows_of(rows_b, chan), own_sem.at[1])
    own_p = pltpu.make_async_copy(send_p.at[last], rows_of(rows_p, chan), own_sem.at[2])
    cov_copy = pltpu.make_async_copy(cov_hbm, cov, cov_sem)

    vis_copy = pltpu.make_async_copy(vis_hbm, vis, vis_sem)
    vis_copy.start()
    barrier = pltpu.get_barrier_semaphore()
    for other in range(1, nx * nz):
        peer = lax.rem(x + other // nz, nx) * nz + lax.rem(z + other % nz, nz)
        pl.semaphore_signal(barrier, inc=1, device_id=(lst, peer), device_id_type=MESH)
    for dl in range(1, nl):
        pl.semaphore_signal(
            barrier, inc=1, device_id=(lax.rem(lst + dl, nl), chan), device_id_type=MESH
        )

    low = lax.broadcasted_iota(jnp.int32, (width, LANES), 1) < held
    lane = lax.broadcasted_iota(jnp.int32, (1, wide), 1)
    spot = lax.broadcasted_iota(jnp.int32, (held, LANES), 0).astype(F32).astype(BF16)
    row_id = lax.broadcasted_iota(jnp.int32, (nx * held, nx * held), 0)
    col_id = lax.broadcasted_iota(jnp.int32, (nx * held, nx * held), 1)
    before = one_if((row_id // held == col_id // held) & (col_id < row_id))
    one, none = jnp.ones((held, LANES), BF16), jnp.zeros((held, LANES), BF16)

    def members(start, live, pooled):
        def spread_out(member, w, offset):
            at = lax.broadcasted_iota(jnp.int32, (held, w), 1) + offset
            mine = one_if((at >= start) & (at < start + live))
            empty = jnp.zeros((held, w), BF16)
            member[pl.ds(0, held), :] = jnp.concatenate([mine, empty], axis=1)
            member[pl.ds(held, held), :] = jnp.concatenate([empty, mine], axis=1)

        spread_out(member_h, LANES, 0)
        spread_out(member_a, rest, LANES)
        at = lax.broadcasted_iota(jnp.int32, (held, LANES), 1)
        below = at < held
        near = lax.rem(at, held) + cap
        mine = (near >= start) & (near < start + live)
        member_b[pl.ds(0, held), :] = one_if(mine & below)
        member_b[pl.ds(held, held), :] = one_if(mine & jnp.logical_not(below))
        far = at + base - pooled
        mine = one_if((far >= jnp.maximum(start, base)) & (far < start + live))
        empty = jnp.zeros((held, LANES), BF16)
        member_p[pl.ds(0, held), :] = jnp.concatenate([mine, empty], axis=1)
        member_p[pl.ds(held, held), :] = jnp.concatenate([empty, mine], axis=1)
        row_id = lax.broadcasted_iota(jnp.int32, (held, LANES), 0)
        lane = lax.rem(lax.broadcasted_iota(jnp.int32, (held, LANES), 1), held)
        spread = jnp.where(row_id == lane, jnp.broadcast_to(live, (held, LANES)), 0)
        count = jnp.sum(spread.astype(F32), axis=0, keepdims=True)
        scale_ref[...] = jnp.broadcast_to(1.0 / (count * (count - 1.0)), scale_ref.shape)

    def column(q, first):
        groups = owner_ref.shape[1]
        lives = []
        for i in range(nx):
            seat = owner_ref[...] - place(q, i) * held
            seat = jnp.where((seat >= 0) & (seat < held), seat, -1).astype(F32).astype(BF16)
            sized = size_ref[...].astype(F32).astype(BF16)
            live_sum = none
            for g in range(0, groups, LANES):
                hit = jnp.broadcast_to(seat[:, g : g + LANES], (held, LANES)) == spot
                pick[pl.ds(i * held, held), pl.ds(g, LANES)] = jnp.where(hit, one, none)
                sizes_here = jnp.broadcast_to(sized[:, g : g + LANES], (held, LANES))
                live_sum += jnp.where(hit, sizes_here, none)
            lives.append(jnp.sum(live_sum.astype(F32), axis=1, keepdims=True))
        live = jnp.concatenate(lives, axis=0)
        if not first:
            for i in range(nx - 1):

                @pl.when(q > 1)
                def _():
                    h_copy(q - 1, i).start()

            h_copy(q - 1, nx - 1).start()
            p_copy(q - 1).start()

            @pl.when(q <= nz // 2)
            def _():
                for i in range(nx):
                    a_copy(q - 1, i).start()

        live_wide = jnp.broadcast_to(live, (nx * held, LANES)).astype(BF16)
        start = dot(before, live_wide)[:, :1].astype(jnp.int32)
        live = live.astype(jnp.int32)
        if first:
            vis_copy.wait()
            cov_copy.start()
        gathered[...] = dot(vis[...], pick[...], NT)
        for i in range(nx):
            for c in range(2):
                for pair in range(SLOT // 2):
                    r0 = (c * SLOT + 2 * pair) * width
                    lanes = pl.ds((i // 2) * LANES, LANES)
                    left = gathered[pl.ds(r0, width), lanes]
                    right = gathered[pl.ds(r0 + width, width), lanes]
                    if i % 2 == 0:
                        joined = jnp.where(low, left, pltpu.roll(right, held, 1))
                    else:
                        joined = jnp.where(low, pltpu.roll(left, held, 1), right)
                    paired[i, pl.ds(c * width, width), pl.ds(pair * LANES, LANES)] = (
                        joined.astype(BF16)
                    )
        ends = (start + live).reshape(nx, held, 1)
        over = [jnp.maximum(ends[i, held - 1 : held] - base, 0) for i in range(nx)]
        pool = None
        for i in range(nx):
            pooled = jnp.zeros((1, 1), jnp.int32)
            for j in range(nx):
                if j != i:
                    ahead_of = lax.rem(x + j, nx) < lax.rem(x + i, nx)
                    pooled += jnp.where(ahead_of, over[j], 0)
            live_i = live[i * held : (i + 1) * held]
            start_i = start[i * held : (i + 1) * held]
            far = lane - (cap + LANES)
            far = jnp.where(far >= pooled, far - pooled + base, -1)
            rank = jnp.where(lane < cap + LANES, jnp.where(lane < base, lane, -1), far)
            slot = rank - start_i
            slot = jnp.where((slot < live_i) & (rank >= 0), slot, -1).astype(F32).astype(BF16)
            for s in range(SLOT):
                chosen[i, pl.ds(s * held, held), :] = jnp.where(
                    slot == float(s), jnp.ones_like(slot), jnp.zeros_like(slot)
                )
            block = dot(paired[i], chosen[i])
            if i == 0:
                held_ref[0] = jnp.broadcast_to(live_i, (held, LANES))
                held_ref[1] = jnp.broadcast_to(start_i, (held, LANES))
                held_ref[2] = jnp.broadcast_to(pooled, (held, LANES))
            n = nx * q + i
            send_h[n, :, pl.ds(0, LANES)] = block[:width, :LANES].astype(BF16)
            send_h[n, :, pl.ds(LANES, LANES)] = block[width:, :LANES].astype(BF16)
            send_a[n, :, pl.ds(0, rest)] = block[:width, LANES:cap].astype(BF16)
            send_a[n, :, pl.ds(rest, rest)] = block[width:, LANES:cap].astype(BF16)
            re, im = block[:width, cap : cap + LANES], block[width:, cap : cap + LANES]
            send_b[n] = jnp.where(low, re, pltpu.roll(im, held, 1)).astype(BF16)
            extra = block[:, cap + LANES :]
            pool = extra if pool is None else pool + extra
        send_p[q, :, pl.ds(0, LANES)] = pool[:width].astype(BF16)
        send_p[q, :, pl.ds(LANES, LANES)] = pool[width:].astype(BF16)

    column(0, True)
    pl.semaphore_wait(barrier, nx * nz - 1 + nl - 1)
    for i in range(nx - 1):
        h_copy(0, i).start()

    def later(q, carry):
        column(q, False)
        return carry

    lax.fori_loop(1, nz, later, 0)
    bin_send[...] = jnp.full(bin_send.shape, bin_ref[0], jnp.int32).astype(F32).astype(BF16)
    for i in range(1, nx):
        h_copy(last, i).start()
    own_h.start()
    own_a.start()
    own_b.start()
    own_p.start()

    def await_all(like, semaphore):
        pltpu.make_async_copy(like, like, semaphore).wait()

    blocks = nx * nz - 1
    def second_rows(q, carry):
        for i in range(nx):
            a_copy(q, i).start()
        return carry

    lax.fori_loop(nz // 2, last, second_rows, 0)
    for i in range(1, nx):
        a_copy(last, i).start()
    for i in (1, 2, 3, 0):

        def start_b(q, carry):
            b_copy(q, i).start()
            return carry

        lax.fori_loop(0, nz - (i == 0), start_b, 0)
    members(held_ref[1][:, :1], held_ref[0][:, :1], held_ref[2][:1, :1])

    def bin_copy(dl):
        return pltpu.make_async_remote_copy(
            src_ref=bin_send,
            dst_ref=bin_land.at[lst],
            send_sem=n_send,
            recv_sem=n_recv,
            device_id=(lax.rem(lst + dl, nl), chan),
            device_id_type=MESH,
        )

    for dl in range(1, nl):
        bin_copy(dl).start()
    bin_land[lst] = bin_send[...]

    steps = step_cos.shape[0]
    bases = half // steps
    unit = 2.0 * math.pi / channels
    shape = (16, channels)
    bit = lax.broadcasted_iota(jnp.int32, shape, 0)
    f = lax.broadcasted_iota(jnp.int32, shape, 1).astype(F32)
    power = jnp.zeros(shape, F32)
    for n in range(10):
        power = jnp.where(bit == n, float(2**n), power)
    product = power * f
    angle = (product - jnp.floor(product * (1.0 / channels)) * channels) * unit
    bit_cos, bit_sin = jnp.cos(angle), jnp.sin(angle)
    shape = (8, channels)
    within = lax.broadcasted_iota(jnp.int32, shape, 0)

    def turned_by(v, n):
        c, s = bit_cos[n : n + 1], bit_sin[n : n + 1]
        return v[0] * c - v[1] * s, v[1] * c + v[0] * s

    def eight(low_bit, v):
        for n in range(3):
            w = turned_by(v, low_bit + n)
            on = (within // 2**n) % 2 == 1
            v = tuple(jnp.where(on, new, old) for new, old in zip(w, v))
        return v

    tiles = [eight(0, (jnp.ones(shape, F32), jnp.zeros(shape, F32)))]
    for n in range(3, 6):
        tiles += [turned_by(v, n) for v in tiles]
    for n, v in enumerate(tiles):
        step_cos[pl.ds(8 * n, 8), :], step_sin[pl.ds(8 * n, 8), :] = v
    f = f[:8] * unit
    taper = (
        0.35875
        - 0.48829 * bit_cos[:1]
        + 0.14128 * bit_cos[1:2]
        - 0.01168 * jnp.cos(3.0 * f)[:1]
    ) * (2.0 / math.sqrt(channels))
    v = eight(6, (jnp.broadcast_to(taper, shape), jnp.zeros(shape, F32)))
    base_cos[pl.ds(0, 8), :], base_sin[pl.ds(0, 8), :] = v
    base_cos[pl.ds(8, 8), :], base_sin[pl.ds(8, 8), :] = turned_by(v, 9)
    channel = lax.broadcasted_iota(jnp.int32, (1, channels), 1)
    middle = taper * jnp.where(channel % 2 == 0, 1.0, -1.0)
    step_row = lax.broadcasted_iota(jnp.int32, (steps, channels), 0)

    def tables(a, carry):
        bc, bs = base_cos[pl.ds(a, 1), :], base_sin[pl.ds(a, 1), :]
        uc, us = step_cos[...], step_sin[...]
        at = pl.multiple_of(a * steps, steps)
        table[pl.ds(at, steps), :] = (uc * bc - us * bs).astype(BF16)
        sines = jnp.where(step_row + at == 0, middle, us * bc + uc * bs)
        table[pl.ds(half + at, steps), :] = sines.astype(BF16)
        return carry

    lax.fori_loop(0, bases, tables, 0)
    cov_copy.wait()
    tall = 256

    def folding(i, carry):
        at = pl.ds(pl.multiple_of(i * tall, tall), tall)
        fold[at, :] = dot(table[at, :], cov[...]).astype(BF16)
        return carry

    folds = channels // tall
    ahead_folds = folds - nz // 2
    lax.fori_loop(0, ahead_folds, folding, 0)

    def pass_on(q):
        for j in range(1, nx):
            f_copy(q, j).start()

    def folding_on(i, carry):
        q = 2 * (i - ahead_folds)
        p_copy(q).wait_recv()
        pass_on(q)

        @pl.when(q + 1 < last)
        def _():
            p_copy(q + 1).wait_recv()

        @pl.when(q + 1 == last)
        def _():
            own_p.wait()

        pass_on(q + 1)
        return folding(i, carry)

    lax.fori_loop(ahead_folds, folds, folding_on, 0)

    def swap(v, w):
        if w < LANES:
            return pltpu.roll(v, w, 1)
        return jnp.concatenate([v[:, w:], v[:, :w]], axis=1)

    def partial(h, rows, member, w):
        at = h * part if isinstance(h, int) else pl.multiple_of(h * part, part)
        if rows is None:
            c = acc_b[pl.ds(at, part), :]
            s = acc_b[pl.ds(half + at, part), :]
        else:
            c = dot(fold[pl.ds(at, part), :], rows[...])
            s = dot(fold[pl.ds(half + at, part), :], rows[...])
        first = lax.broadcasted_iota(jnp.int32, (part, 1), 0) + at == 0
        mine = member[...]

        def total(v):
            return dot(v, mine, NT)

        def exact(v):
            top = v.astype(BF16)
            return total(top) + total((v - top.astype(F32)).astype(BF16))

        if w < LANES:
            cr, sr = swap(c, w), swap(s, w)
            even, odd = c * c + cr * cr, s * s + sr * sr
            cross = 2.0 * (c * sr - cr * s)
            lane = lax.broadcasted_iota(jnp.int32, (1, 2 * w), 1)
            powers = jnp.where(first, jnp.where(lane < w, even, odd), even + odd + cross)
        else:
            rc, ic, rs, im = c[:, :w], c[:, w:], s[:, :w], s[:, w:]
            even, odd = rc * rc + ic * ic, rs * rs + im * im
            cross = 2.0 * (rc * im - ic * rs)
            powers = jnp.concatenate(
                [jnp.where(first, even, even + odd + cross), jnp.where(first, odd, even + odd - cross)],
                axis=1,
            )
        return exact(c), exact(s), total(powers.astype(BF16)), first

    own_h.wait()
    await_all(send_h.at[pl.ds(0, blocks)], h_recv)

    def part_h(h, carry):
        at = pl.ds(pl.multiple_of(h * part, part), part)
        for n, v in enumerate(partial(h, rows_h, member_h, LANES)[:3]):
            sums[n, at, :] = v
        return carry

    lax.fori_loop(0, spans, part_h, 0)
    own_a.wait()
    await_all(send_a.at[pl.ds(0, blocks)], a_recv)

    def part_a(h, carry):
        at = pl.ds(pl.multiple_of(h * part, part), part)
        for n, v in enumerate(partial(h, rows_a, member_a, rest)[:3]):
            sums[n, at, :] += v
        return carry

    lax.fori_loop(0, spans, part_a, 0)
    relayed = rows_p.at[pl.ds(0, nz * (nx - 1) * width), :]
    await_all(relayed, f_recv)

    def part_p(h, carry):
        at = pl.ds(pl.multiple_of(h * part, part), part)
        for n, v in enumerate(partial(h, rows_p, member_p, LANES)[:3]):
            sums[n, at, :] += v
        return carry

    lax.fori_loop(0, spans, part_p, 0)
    await_all(send_h.at[pl.ds(0, blocks)], h_send)
    await_all(send_a.at[pl.ds(0, blocks)], a_send)
    await_all(send_p.at[pl.ds(0, last)], p_send)
    await_all(relayed, f_send)
    await_all(bin_land.at[pl.ds(0, nl - 1)], n_send)
    await_all(bin_land.at[pl.ds(0, nl - 1)], n_recv)
    deep = nz * width
    for i in (1, 2, 3, 0):
        await_all(send_b.at[pl.ds(0, nz - (i == 0))], b_recv.at[i])
        if i == 0:
            own_b.wait()
        ch = pl.ds(pl.multiple_of(lax.rem(x + nx - i, nx) * deep, deep), deep)
        term = dot(fold[:, ch], rows_b[ch, :])
        if i == 1:
            acc_b[...] = term
        else:
            acc_b[...] += term

    def share_copy(source, h, to):
        return pltpu.make_async_remote_copy(
            src_ref=source.at[h],
            dst_ref=landed.at[lst],
            send_sem=y_send,
            recv_sem=y_recv,
            device_id=(to, chan),
            device_id_type=MESH,
        )

    def share(source, h, to):
        @pl.when(to != lst)
        def _():
            share_copy(source, h, to).start()

        @pl.when(to == lst)
        def _():
            landed[lst] = source[h]

    tall_share = part // 2
    below = lax.broadcasted_iota(jnp.int32, (part, LANES), 1) < held
    for h in range(spans):
        share_plus[h, pl.ds(tall_share, TAIL), :] = jnp.zeros((TAIL, LANES), BF16)

    def finish(h):
        at = pl.ds(h * part, part)
        c, s, p, first = partial(h, None, member_b, held)
        c, s, p = c + sums[0, at, :], s + sums[1, at, :], p + sums[2, at, :]
        turned = jnp.where(below, 1.0, -1.0) * pltpu.roll(s, held, 1)
        up = jnp.where(first, c, c + turned)
        down = jnp.where(first, s, c - turned)
        up, down = up * up, down * down
        whole = jnp.where(below, up + pltpu.roll(up, held, 1), down + pltpu.roll(down, held, 1))
        crossed = (whole - p) * scale_ref[:1, :]
        top, bottom = crossed[:tall_share], crossed[tall_share:]
        under = below[:tall_share]
        share_plus[h, pl.ds(0, tall_share), :] = jnp.where(
            under, top, pltpu.roll(bottom, held, 1)
        ).astype(BF16)
        minus = jnp.where(under, pltpu.roll(top, held, 1), bottom).astype(BF16)
        share_minus[h, pl.ds(0, tall_share), :] = minus

        share_minus[(h - 1) % spans, pl.ds(tall_share, TAIL), :] = minus[:TAIL]

    for h in range(spans):
        if h == 2:
            share(share_plus, 0, 0)
            share(share_plus, 1, 1)
            share(share_minus, 0, nl - 1)
        finish(h)
    for h in range(2, spans):
        share(share_plus, h, h)
    for h in range(1, spans):
        share(share_minus, h, nl - 1 - h)

    row = lax.broadcasted_iota(jnp.int32, (tall_share + TAIL, part), 0)
    col = lax.broadcasted_iota(jnp.int32, (tall_share + TAIL, part), 1)
    want = jnp.where(lst < spans, col, part - col)
    lower = one_if((row == want) & (row < tall_share) | (row == want - tall_share) & (want == part))
    upper = one_if((row + tall_share == want) & (row < tall_share))
    turn = jnp.concatenate([lower, upper], axis=1)

    def order(t):
        both = dot(landed[t], turn, TN)
        pieces[t] = both[:held, :part] + both[held:, part:]

    await_all(send_b.at[pl.ds(0, blocks)], b_send)
    order(lst)
    await_all(landed.at[pl.ds(0, nl - 1)], y_recv)
    for dl in range(1, nl):
        order(lax.rem(lst + dl, nl))
    codes = [bin_land[t].astype(F32)[:1, :1] for t in range(nl)]
    for b in range(NBIN):
        total = jnp.zeros((held, part), F32)
        count = jnp.zeros((1, 1), F32)
        for t in range(nl):
            inside = codes[t] == b
            total += jnp.where(inside, pieces[t], 0.0)
            count += jnp.where(inside, 1.0, 0.0)
        out_ref[b] = total * (1.0 / jnp.maximum(count, 1.0))

    await_all(landed.at[pl.ds(0, nl - 1)], y_send)


def cross_power(cap, collective_id, sizes, lst_bin, owner, size, vis, cov):
    nx, nz, nl, held, channels, width = sizes
    half = channels // 2
    part = channels // nl
    total = nx * nz
    vmem = pltpu.VMEM
    dma = pltpu.SemaphoreType.DMA
    share = (channels // (2 * part), part // 2 + TAIL, LANES)
    return pl.pallas_call(
        functools.partial(kernel, cap, sizes),
        out_shape=jax.ShapeDtypeStruct((NBIN, held, part), F32),
        in_specs=[
            pl.BlockSpec(memory_space=pltpu.SMEM),
            pl.BlockSpec(memory_space=vmem),
            pl.BlockSpec(memory_space=vmem),
            pl.BlockSpec(memory_space=pl.ANY),
            pl.BlockSpec(memory_space=pl.ANY),
        ],
        out_specs=pl.BlockSpec(memory_space=vmem),
        scratch_shapes=[
            vmem(vis.shape, BF16),
            dma(()),
            vmem((channels, channels), BF16),
            vmem((nx * held, owner.shape[1]), BF16),
            vmem((nx, SLOT * held, cap + 2 * LANES), BF16),
            vmem((2 * SLOT * width, nx * held), F32),
            vmem((nx, 2 * width, SLOT * held), BF16),
            vmem((total, width, 2 * LANES), BF16),
            vmem((total, width, 2 * (cap - LANES)), BF16),
            vmem((total, width, LANES), BF16),
            vmem((nz, width, 2 * LANES), BF16),
            vmem((channels, 2 * LANES), BF16),
            vmem((channels, 2 * (cap - LANES)), BF16),
            vmem((channels, LANES), BF16),
            vmem((channels, 2 * LANES), BF16),
            vmem((channels, channels), BF16),
            vmem((channels, channels), BF16),
            vmem((64, channels), F32),
            vmem((64, channels), F32),
            vmem((16, channels), F32),
            vmem((16, channels), F32),
            vmem((2 * held, 2 * LANES), BF16),
            vmem((2 * held, 2 * (cap - LANES)), BF16),
            vmem((2 * held, LANES), BF16),
            vmem((2 * held, 2 * LANES), BF16),
            vmem((8, LANES), F32),
            vmem((3, held, LANES), jnp.int32),
            vmem((3, half, LANES), F32),
            vmem((channels, LANES), F32),
            vmem(share, BF16),
            vmem(share, BF16),
            vmem((nl,) + share[1:], BF16),
            vmem((nl, held, part), F32),
            vmem((16, LANES), BF16),
            vmem((nl, 16, LANES), BF16),
            dma(()),
            dma((4,)),
            dma(()),
            dma(()),
            dma(()),
            dma(()),
            dma(()),
            dma((nx,)),
            dma(()),
            dma((nz,)),
            dma(()),
            dma(()),
            dma(()),
            dma(()),
            dma(()),
            dma(()),
        ],
        compiler_params=pltpu.CompilerParams(
            collective_id=collective_id, has_side_effects=True, vmem_limit_bytes=60 * 2**20
        ),
    )(lst_bin, owner, size, vis, cov)


def solution(mesh):
    nl, total = mesh.shape["lst"], mesh.shape["chan"]
    nx = total // 8
    nz = total // nx

    def shards(visibility, inverse_cov, group_size, group_owner, lst_bin):
        groups, width = visibility.shape[2], visibility.shape[4]
        channels = inverse_cov.shape[0]
        held = groups // total
        sizes = (nx, nz, nl, held, channels, width)
        vis = jnp.transpose(visibility, (0, 1, 3, 4, 2)).reshape(2 * SLOT * width, groups)
        owner = group_owner.reshape(1, groups)
        size = group_size.reshape(1, groups)
        full = SLOT * held
        tight = full // 2
        fits = pl.pallas_call(
            functools.partial(fits_kernel, tight + held, LANES, sizes),
            out_shape=jax.ShapeDtypeStruct((1,), jnp.int32),
            out_specs=pl.BlockSpec(memory_space=pltpu.SMEM),
        )(owner, size)
        return lax.cond(
            fits[0] > 0,
            functools.partial(cross_power, tight, 0, sizes),
            functools.partial(cross_power, full, 1, sizes),
            lst_bin, owner, size, vis, inverse_cov,
        )

    placed = (P(None, "lst", None, None, "chan"), P(), P(), P(), P("lst"))
    return jax.shard_map(
        shards, mesh=mesh, in_specs=placed, out_specs=P(None, "chan", "lst"), check_vma=False
    )
```

```python
import functools
import math

import jax
import jax.numpy as jnp
from jax import lax
from jax.experimental import pallas as pl
from jax.experimental.pallas import tpu as pltpu
from jax.sharding import PartitionSpec as P

NBIN = 8
SLOT = 8
MESH = pl.DeviceIdType.MESH
F32 = jnp.float32
BF16 = jnp.bfloat16
NN = (((1,), (0,)), ((), ()))
NT = (((1,), (1,)), ((), ()))
TN = (((0,), (0,)), ((), ()))
TAIL = 16
LANES = 128


def dot(a, b, dims=NN):
    return lax.dot_general(a, b, dims, preferred_element_type=F32)


def one_if(condition):
    return jnp.where(condition, 1.0, 0.0).astype(BF16)


def fits_kernel(base, room, sizes, owner_ref, size_ref, out_ref):
    nx, nz, nl, held, channels, width = sizes
    first = lax.broadcasted_iota(jnp.int32, (nx * nz, 1), 0) * held
    owner = owner_ref[...]
    mine = (owner >= first) & (owner < first + held)
    lives = jnp.sum(jnp.where(mine, size_ref[...], 0), axis=1, keepdims=True)
    over = jnp.maximum(lives - base, 0).reshape(nx, nz, 1)
    out_ref[0] = jnp.where(jnp.max(jnp.sum(over, axis=0)) <= room, 1, 0)


def kernel(
    cap,
    sizes,
    bin_ref,
    owner_ref,
    size_ref,
    vis_hbm,
    cov_hbm,
    out_ref,
    vis,
    vis_sem,
    cov,
    pick,
    chosen,
    gathered,
    paired,
    send_h,
    send_a,
    send_b,
    send_p,
    rows_h,
    rows_a,
    rows_b,
    rows_p,
    table,
    fold,
    step_cos,
    step_sin,
    base_cos,
    base_sin,
    member_h,
    member_a,
    member_b,
    member_p,
    scale_ref,
    held_ref,
    sums,
    acc_b,
    share_plus,
    share_minus,
    landed,
    pieces,
    bin_send,
    bin_land,
    cov_sem,
    own_sem,
    h_send,
    h_recv,
    a_send,
    a_recv,
    b_send,
    b_recv,
    p_send,
    p_recv,
    f_send,
    f_recv,
    y_send,
    y_recv,
    n_send,
    n_recv,
):
    nx, nz, nl, held, channels, width = sizes
    half = channels // 2
    part = channels // nl
    spans = half // part
    base = cap + held
    wide = cap + 2 * LANES
    rest = cap - LANES
    lst = lax.axis_index("lst")
    chan = lax.axis_index("chan")
    x, z = chan // nz, chan % nz
    last = nz - 1
    early = 1

    def ahead(q):
        return nz // 2 + (1 - 2 * (q % 2)) * ((q + 1) // 2)

    def place(q, i):
        return lax.rem(x + i, nx) * nz + lax.rem(z + ahead(q), nz)

    def rows_of(ref, source):
        return ref.at[pl.ds(pl.multiple_of(source * width, 16), width), :]

    def h_copy(q, i):
        n = nx * q + i
        return pltpu.make_async_remote_copy(
            src_ref=send_h.at[n],
            dst_ref=rows_of(rows_h, chan),
            send_sem=h_send,
            recv_sem=h_recv,
            device_id=(lst, place(q, i)),
            device_id_type=MESH,
        )

    def a_copy(q, i):
        n = nx * q + i
        return pltpu.make_async_remote_copy(
            src_ref=send_a.at[n],
            dst_ref=rows_of(rows_a, chan),
            send_sem=a_send,
            recv_sem=a_recv,
            device_id=(lst, place(q, i)),
            device_id_type=MESH,
        )

    def b_copy(q, i):
        n = nx * q + i
        return pltpu.make_async_remote_copy(
            src_ref=send_b.at[n],
            dst_ref=rows_of(rows_b, chan),
            send_sem=b_send,
            recv_sem=b_recv.at[i],
            device_id=(lst, place(q, i)),
            device_id_type=MESH,
        )

    def p_copy(q):
        return pltpu.make_async_remote_copy(
            src_ref=send_p.at[q],
            dst_ref=rows_of(rows_p, chan),
            send_sem=p_send,
            recv_sem=p_recv.at[q],
            device_id=(lst, place(q, 0)),
            device_id_type=MESH,
        )

    def f_copy(q, j):
        source = x * nz + lax.rem(z + nz - ahead(q), nz)
        return pltpu.make_async_remote_copy(
            src_ref=rows_of(rows_p, source),
            dst_ref=rows_of(rows_p, source),
            send_sem=f_send,
            recv_sem=f_recv,
            device_id=(lst, lax.rem(x + j, nx) * nz + z),
            device_id_type=MESH,
        )

    own_h = pltpu.make_async_copy(send_h.at[nx * last], rows_of(rows_h, chan), own_sem.at[3])
    own_a = pltpu.make_async_copy(send_a.at[nx * last], rows_of(rows_a, chan), own_sem.at[0])
    own_b = pltpu.make_async_copy(send_b.at[nx * last], rows_of(rows_b, chan), own_sem.at[1])
    own_p = pltpu.make_async_copy(send_p.at[last], rows_of(rows_p, chan), own_sem.at[2])
    cov_copy = pltpu.make_async_copy(cov_hbm, cov, cov_sem)

    vis_copy = pltpu.make_async_copy(vis_hbm, vis, vis_sem)
    vis_copy.start()
    barrier = pltpu.get_barrier_semaphore()
    for other in range(1, nx * nz):
        peer = lax.rem(x + other // nz, nx) * nz + lax.rem(z + other % nz, nz)
        pl.semaphore_signal(barrier, inc=1, device_id=(lst, peer), device_id_type=MESH)
    for dl in range(1, nl):
        pl.semaphore_signal(
            barrier, inc=1, device_id=(lax.rem(lst + dl, nl), chan), device_id_type=MESH
        )

    low = lax.broadcasted_iota(jnp.int32, (width, LANES), 1) < held
    lane = lax.broadcasted_iota(jnp.int32, (1, wide), 1)
    spot = lax.broadcasted_iota(jnp.int32, (held, LANES), 0).astype(F32).astype(BF16)
    row_id = lax.broadcasted_iota(jnp.int32, (nx * held, nx * held), 0)
    col_id = lax.broadcasted_iota(jnp.int32, (nx * held, nx * held), 1)
    before = one_if((row_id // held == col_id // held) & (col_id < row_id))
    one, none = jnp.ones((held, LANES), BF16), jnp.zeros((held, LANES), BF16)

    def members(start, live, pooled):
        def spread_out(member, w, offset):
            at = lax.broadcasted_iota(jnp.int32, (held, w), 1) + offset
            mine = one_if((at >= start) & (at < start + live))
            empty = jnp.zeros((held, w), BF16)
            member[pl.ds(0, held), :] = jnp.concatenate([mine, empty], axis=1)
            member[pl.ds(held, held), :] = jnp.concatenate([empty, mine], axis=1)

        spread_out(member_h, LANES, 0)
        spread_out(member_a, rest, LANES)
        at = lax.broadcasted_iota(jnp.int32, (held, LANES), 1)
        below = at < held
        near = lax.rem(at, held) + cap
        mine = (near >= start) & (near < start + live)
        member_b[pl.ds(0, held), :] = one_if(mine & below)
        member_b[pl.ds(held, held), :] = one_if(mine & jnp.logical_not(below))
        far = at + base - pooled
        mine = one_if((far >= jnp.maximum(start, base)) & (far < start + live))
        empty = jnp.zeros((held, LANES), BF16)
        member_p[pl.ds(0, held), :] = jnp.concatenate([mine, empty], axis=1)
        member_p[pl.ds(held, held), :] = jnp.concatenate([empty, mine], axis=1)
        row_id = lax.broadcasted_iota(jnp.int32, (held, LANES), 0)
        lane = lax.rem(lax.broadcasted_iota(jnp.int32, (held, LANES), 1), held)
        spread = jnp.where(row_id == lane, jnp.broadcast_to(live, (held, LANES)), 0)
        count = jnp.sum(spread.astype(F32), axis=0, keepdims=True)
        scale_ref[...] = jnp.broadcast_to(1.0 / (count * (count - 1.0)), scale_ref.shape)

    def column(q, first):
        groups = owner_ref.shape[1]
        lives = []
        for i in range(nx):
            seat = owner_ref[...] - place(q, i) * held
            seat = jnp.where((seat >= 0) & (seat < held), seat, -1).astype(F32).astype(BF16)
            sized = size_ref[...].astype(F32).astype(BF16)
            live_sum = none
            for g in range(0, groups, LANES):
                hit = jnp.broadcast_to(seat[:, g : g + LANES], (held, LANES)) == spot
                pick[pl.ds(i * held, held), pl.ds(g, LANES)] = jnp.where(hit, one, none)
                sizes_here = jnp.broadcast_to(sized[:, g : g + LANES], (held, LANES))
                live_sum += jnp.where(hit, sizes_here, none)
            lives.append(jnp.sum(live_sum.astype(F32), axis=1, keepdims=True))
        live = jnp.concatenate(lives, axis=0)
        if not first:
            for i in range(nx - 1):

                @pl.when(q > 1)
                def _():
                    h_copy(q - 1, i).start()

            h_copy(q - 1, nx - 1).start()
            p_copy(q - 1).start()

            @pl.when(q <= early)
            def _():
                for i in range(nx):
                    a_copy(q - 1, i).start()

        live_wide = jnp.broadcast_to(live, (nx * held, LANES)).astype(BF16)
        start = dot(before, live_wide)[:, :1].astype(jnp.int32)
        live = live.astype(jnp.int32)
        if first:
            vis_copy.wait()
            cov_copy.start()
        gathered[...] = dot(vis[...], pick[...], NT)
        for i in range(nx):
            for c in range(2):
                for pair in range(SLOT // 2):
                    r0 = (c * SLOT + 2 * pair) * width
                    lanes = pl.ds((i // 2) * LANES, LANES)
                    left = gathered[pl.ds(r0, width), lanes]
                    right = gathered[pl.ds(r0 + width, width), lanes]
                    if i % 2 == 0:
                        joined = jnp.where(low, left, pltpu.roll(right, held, 1))
                    else:
                        joined = jnp.where(low, pltpu.roll(left, held, 1), right)
                    paired[i, pl.ds(c * width, width), pl.ds(pair * LANES, LANES)] = (
                        joined.astype(BF16)
                    )
        ends = (start + live).reshape(nx, held, 1)
        over = [jnp.maximum(ends[i, held - 1 : held] - base, 0) for i in range(nx)]
        pool = None
        for i in range(nx):
            pooled = jnp.zeros((1, 1), jnp.int32)
            for j in range(nx):
                if j != i:
                    ahead_of = lax.rem(x + j, nx) < lax.rem(x + i, nx)
                    pooled += jnp.where(ahead_of, over[j], 0)
            live_i = live[i * held : (i + 1) * held]
            start_i = start[i * held : (i + 1) * held]
            far = lane - (cap + LANES)
            far = jnp.where(far >= pooled, far - pooled + base, -1)
            rank = jnp.where(lane < cap + LANES, jnp.where(lane < base, lane, -1), far)
            slot = rank - start_i
            slot = jnp.where((slot < live_i) & (rank >= 0), slot, -1).astype(F32).astype(BF16)
            for s in range(SLOT):
                chosen[i, pl.ds(s * held, held), :] = jnp.where(
                    slot == float(s), jnp.ones_like(slot), jnp.zeros_like(slot)
                )
            block = dot(paired[i], chosen[i])
            if i == 0:
                held_ref[0] = jnp.broadcast_to(live_i, (held, LANES))
                held_ref[1] = jnp.broadcast_to(start_i, (held, LANES))
                held_ref[2] = jnp.broadcast_to(pooled, (held, LANES))
            n = nx * q + i
            send_h[n, :, pl.ds(0, LANES)] = block[:width, :LANES].astype(BF16)
            send_h[n, :, pl.ds(LANES, LANES)] = block[width:, :LANES].astype(BF16)
            send_a[n, :, pl.ds(0, rest)] = block[:width, LANES:cap].astype(BF16)
            send_a[n, :, pl.ds(rest, rest)] = block[width:, LANES:cap].astype(BF16)
            re, im = block[:width, cap : cap + LANES], block[width:, cap : cap + LANES]
            send_b[n] = jnp.where(low, re, pltpu.roll(im, held, 1)).astype(BF16)
            extra = block[:, cap + LANES :]
            pool = extra if pool is None else pool + extra
        send_p[q, :, pl.ds(0, LANES)] = pool[:width].astype(BF16)
        send_p[q, :, pl.ds(LANES, LANES)] = pool[width:].astype(BF16)

    column(0, True)
    pl.semaphore_wait(barrier, nx * nz - 1 + nl - 1)
    for i in range(nx - 1):
        h_copy(0, i).start()

    def later(q, carry):
        column(q, False)
        return carry

    lax.fori_loop(1, nz, later, 0)
    bin_send[...] = jnp.full(bin_send.shape, bin_ref[0], jnp.int32).astype(F32).astype(BF16)
    for i in range(1, nx):
        h_copy(last, i).start()
    own_h.start()
    own_a.start()
    own_b.start()
    own_p.start()

    def await_all(like, semaphore):
        pltpu.make_async_copy(like, like, semaphore).wait()

    blocks = nx * nz - 1
    def second_rows(q, carry):
        for i in range(nx):
            a_copy(q, i).start()
        return carry

    lax.fori_loop(early, last, second_rows, 0)
    for i in range(1, nx):
        a_copy(last, i).start()
    for i in (1, 2, 3, 0):

        def start_b(q, carry):
            b_copy(q, i).start()
            return carry

        lax.fori_loop(0, nz - (i == 0), start_b, 0)
    members(held_ref[1][:, :1], held_ref[0][:, :1], held_ref[2][:1, :1])

    def bin_copy(dl):
        return pltpu.make_async_remote_copy(
            src_ref=bin_send,
            dst_ref=bin_land.at[lst],
            send_sem=n_send,
            recv_sem=n_recv,
            device_id=(lax.rem(lst + dl, nl), chan),
            device_id_type=MESH,
        )

    for dl in range(1, nl):
        bin_copy(dl).start()
    bin_land[lst] = bin_send[...]

    steps = step_cos.shape[0]
    bases = half // steps
    unit = 2.0 * math.pi / channels
    shape = (16, channels)
    bit = lax.broadcasted_iota(jnp.int32, shape, 0)
    f = lax.broadcasted_iota(jnp.int32, shape, 1).astype(F32)
    power = jnp.zeros(shape, F32)
    for n in range(10):
        power = jnp.where(bit == n, float(2**n), power)
    product = power * f
    angle = (product - jnp.floor(product * (1.0 / channels)) * channels) * unit
    bit_cos, bit_sin = jnp.cos(angle), jnp.sin(angle)
    shape = (8, channels)
    within = lax.broadcasted_iota(jnp.int32, shape, 0)

    def turned_by(v, n):
        c, s = bit_cos[n : n + 1], bit_sin[n : n + 1]
        return v[0] * c - v[1] * s, v[1] * c + v[0] * s

    def eight(low_bit, v):
        for n in range(3):
            w = turned_by(v, low_bit + n)
            on = (within // 2**n) % 2 == 1
            v = tuple(jnp.where(on, new, old) for new, old in zip(w, v))
        return v

    tiles = [eight(0, (jnp.ones(shape, F32), jnp.zeros(shape, F32)))]
    for n in range(3, 6):
        tiles += [turned_by(v, n) for v in tiles]
    for n, v in enumerate(tiles):
        step_cos[pl.ds(8 * n, 8), :], step_sin[pl.ds(8 * n, 8), :] = v
    f = f[:8] * unit
    taper = (
        0.35875
        - 0.48829 * bit_cos[:1]
        + 0.14128 * bit_cos[1:2]
        - 0.01168 * jnp.cos(3.0 * f)[:1]
    ) * (2.0 / math.sqrt(channels))
    v = eight(6, (jnp.broadcast_to(taper, shape), jnp.zeros(shape, F32)))
    base_cos[pl.ds(0, 8), :], base_sin[pl.ds(0, 8), :] = v
    base_cos[pl.ds(8, 8), :], base_sin[pl.ds(8, 8), :] = turned_by(v, 9)
    channel = lax.broadcasted_iota(jnp.int32, (1, channels), 1)
    middle = taper * jnp.where(channel % 2 == 0, 1.0, -1.0)
    step_row = lax.broadcasted_iota(jnp.int32, (steps, channels), 0)

    def tables(a, carry):
        bc, bs = base_cos[pl.ds(a, 1), :], base_sin[pl.ds(a, 1), :]
        uc, us = step_cos[...], step_sin[...]
        at = pl.multiple_of(a * steps, steps)
        table[pl.ds(at, steps), :] = (uc * bc - us * bs).astype(BF16)
        sines = jnp.where(step_row + at == 0, middle, us * bc + uc * bs)
        table[pl.ds(half + at, steps), :] = sines.astype(BF16)
        return carry

    lax.fori_loop(0, bases, tables, 0)
    cov_copy.wait()
    tall = 256

    def folding(i, carry):
        at = pl.ds(pl.multiple_of(i * tall, tall), tall)
        fold[at, :] = dot(table[at, :], cov[...]).astype(BF16)
        return carry

    folds = channels // tall
    ahead_folds = 1
    lax.fori_loop(0, ahead_folds, folding, 0)

    def pass_on(q):
        for j in range(1, nx):
            f_copy(q, j).start()

    def folding_on(i, carry):
        q = 2 * (i - ahead_folds)
        p_copy(q).wait_recv()
        pass_on(q)

        @pl.when(q + 1 < last)
        def _():
            p_copy(q + 1).wait_recv()

        @pl.when(q + 1 == last)
        def _():
            own_p.wait()

        pass_on(q + 1)
        return folding(i, carry)

    passed = ahead_folds + nz // 2
    lax.fori_loop(ahead_folds, passed, folding_on, 0)
    lax.fori_loop(passed, folds, folding, 0)

    def swap(v, w):
        if w < LANES:
            return pltpu.roll(v, w, 1)
        return jnp.concatenate([v[:, w:], v[:, :w]], axis=1)

    def partial(h, rows, member, w):
        at = h * part if isinstance(h, int) else pl.multiple_of(h * part, part)
        if rows is None:
            c = acc_b[pl.ds(at, part), :]
            s = acc_b[pl.ds(half + at, part), :]
        else:
            c = dot(fold[pl.ds(at, part), :], rows[...])
            s = dot(fold[pl.ds(half + at, part), :], rows[...])
        first = lax.broadcasted_iota(jnp.int32, (part, 1), 0) + at == 0
        mine = member[...]

        def total(v):
            return dot(v, mine, NT)

        def exact(v):
            top = v.astype(BF16)
            return total(top) + total((v - top.astype(F32)).astype(BF16))

        if w < LANES:
            cr, sr = swap(c, w), swap(s, w)
            even, odd = c * c + cr * cr, s * s + sr * sr
            cross = 2.0 * (c * sr - cr * s)
            lane = lax.broadcasted_iota(jnp.int32, (1, 2 * w), 1)
            powers = jnp.where(first, jnp.where(lane < w, even, odd), even + odd + cross)
        else:
            rc, ic, rs, im = c[:, :w], c[:, w:], s[:, :w], s[:, w:]
            even, odd = rc * rc + ic * ic, rs * rs + im * im
            cross = 2.0 * (rc * im - ic * rs)
            powers = jnp.concatenate(
                [jnp.where(first, even, even + odd + cross), jnp.where(first, odd, even + odd - cross)],
                axis=1,
            )
        return exact(c), exact(s), total(powers.astype(BF16)), first

    own_h.wait()
    await_all(send_h.at[pl.ds(0, blocks)], h_recv)

    def part_h(h, carry):
        at = pl.ds(pl.multiple_of(h * part, part), part)
        for n, v in enumerate(partial(h, rows_h, member_h, LANES)[:3]):
            sums[n, at, :] = v
        return carry

    lax.fori_loop(0, spans, part_h, 0)
    relayed = rows_p.at[pl.ds(0, nz * (nx - 1) * width), :]
    await_all(relayed, f_recv)

    def part_p(h, carry):
        at = pl.ds(pl.multiple_of(h * part, part), part)
        for n, v in enumerate(partial(h, rows_p, member_p, LANES)[:3]):
            sums[n, at, :] += v
        return carry

    lax.fori_loop(0, spans, part_p, 0)
    own_a.wait()
    await_all(send_a.at[pl.ds(0, blocks)], a_recv)

    def part_a(h, carry):
        at = pl.ds(pl.multiple_of(h * part, part), part)
        for n, v in enumerate(partial(h, rows_a, member_a, rest)[:3]):
            sums[n, at, :] += v
        return carry

    lax.fori_loop(0, spans, part_a, 0)
    await_all(send_h.at[pl.ds(0, blocks)], h_send)
    await_all(send_a.at[pl.ds(0, blocks)], a_send)
    await_all(send_p.at[pl.ds(0, last)], p_send)
    await_all(relayed, f_send)
    await_all(bin_land.at[pl.ds(0, nl - 1)], n_send)
    await_all(bin_land.at[pl.ds(0, nl - 1)], n_recv)
    deep = nz * width
    for i in (1, 2, 3, 0):
        await_all(send_b.at[pl.ds(0, nz - (i == 0))], b_recv.at[i])
        if i == 0:
            own_b.wait()
        ch = pl.ds(pl.multiple_of(lax.rem(x + nx - i, nx) * deep, deep), deep)
        term = dot(fold[:, ch], rows_b[ch, :])
        if i == 1:
            acc_b[...] = term
        else:
            acc_b[...] += term

    def share_copy(source, h, to):
        return pltpu.make_async_remote_copy(
            src_ref=source.at[h],
            dst_ref=landed.at[lst],
            send_sem=y_send,
            recv_sem=y_recv,
            device_id=(to, chan),
            device_id_type=MESH,
        )

    def share(source, h, to):
        @pl.when(to != lst)
        def _():
            share_copy(source, h, to).start()

        @pl.when(to == lst)
        def _():
            landed[lst] = source[h]

    tall_share = part // 2
    below = lax.broadcasted_iota(jnp.int32, (part, LANES), 1) < held
    for h in range(spans):
        share_plus[h, pl.ds(tall_share, TAIL), :] = jnp.zeros((TAIL, LANES), BF16)

    def finish(h):
        at = pl.ds(h * part, part)
        c, s, p, first = partial(h, None, member_b, held)
        c, s, p = c + sums[0, at, :], s + sums[1, at, :], p + sums[2, at, :]
        turned = jnp.where(below, 1.0, -1.0) * pltpu.roll(s, held, 1)
        up = jnp.where(first, c, c + turned)
        down = jnp.where(first, s, c - turned)
        up, down = up * up, down * down
        whole = jnp.where(below, up + pltpu.roll(up, held, 1), down + pltpu.roll(down, held, 1))
        crossed = (whole - p) * scale_ref[:1, :]
        top, bottom = crossed[:tall_share], crossed[tall_share:]
        under = below[:tall_share]
        share_plus[h, pl.ds(0, tall_share), :] = jnp.where(
            under, top, pltpu.roll(bottom, held, 1)
        ).astype(BF16)
        minus = jnp.where(under, pltpu.roll(top, held, 1), bottom).astype(BF16)
        share_minus[h, pl.ds(0, tall_share), :] = minus

        share_minus[(h - 1) % spans, pl.ds(tall_share, TAIL), :] = minus[:TAIL]

    for h in range(spans):
        if h == 2:
            share(share_plus, 0, 0)
            share(share_plus, 1, 1)
            share(share_minus, 0, nl - 1)
        finish(h)
    for h in range(2, spans):
        share(share_plus, h, h)
    for h in range(1, spans):
        share(share_minus, h, nl - 1 - h)

    row = lax.broadcasted_iota(jnp.int32, (tall_share + TAIL, part), 0)
    col = lax.broadcasted_iota(jnp.int32, (tall_share + TAIL, part), 1)
    want = jnp.where(lst < spans, col, part - col)
    lower = one_if((row == want) & (row < tall_share) | (row == want - tall_share) & (want == part))
    upper = one_if((row + tall_share == want) & (row < tall_share))
    turn = jnp.concatenate([lower, upper], axis=1)

    def order(t):
        both = dot(landed[t], turn, TN)
        pieces[t] = both[:held, :part] + both[held:, part:]

    await_all(send_b.at[pl.ds(0, blocks)], b_send)
    order(lst)
    await_all(landed.at[pl.ds(0, nl - 1)], y_recv)
    for dl in range(1, nl):
        order(lax.rem(lst + dl, nl))
    codes = [bin_land[t].astype(F32)[:1, :1] for t in range(nl)]
    for b in range(NBIN):
        total = jnp.zeros((held, part), F32)
        count = jnp.zeros((1, 1), F32)
        for t in range(nl):
            inside = codes[t] == b
            total += jnp.where(inside, pieces[t], 0.0)
            count += jnp.where(inside, 1.0, 0.0)
        out_ref[b] = total * (1.0 / jnp.maximum(count, 1.0))

    await_all(landed.at[pl.ds(0, nl - 1)], y_send)


def cross_power(cap, collective_id, sizes, lst_bin, owner, size, vis, cov):
    nx, nz, nl, held, channels, width = sizes
    half = channels // 2
    part = channels // nl
    total = nx * nz
    vmem = pltpu.VMEM
    dma = pltpu.SemaphoreType.DMA
    share = (channels // (2 * part), part // 2 + TAIL, LANES)
    return pl.pallas_call(
        functools.partial(kernel, cap, sizes),
        out_shape=jax.ShapeDtypeStruct((NBIN, held, part), F32),
        in_specs=[
            pl.BlockSpec(memory_space=pltpu.SMEM),
            pl.BlockSpec(memory_space=vmem),
            pl.BlockSpec(memory_space=vmem),
            pl.BlockSpec(memory_space=pl.ANY),
            pl.BlockSpec(memory_space=pl.ANY),
        ],
        out_specs=pl.BlockSpec(memory_space=vmem),
        scratch_shapes=[
            vmem(vis.shape, BF16),
            dma(()),
            vmem((channels, channels), BF16),
            vmem((nx * held, owner.shape[1]), BF16),
            vmem((nx, SLOT * held, cap + 2 * LANES), BF16),
            vmem((2 * SLOT * width, nx * held), F32),
            vmem((nx, 2 * width, SLOT * held), BF16),
            vmem((total, width, 2 * LANES), BF16),
            vmem((total, width, 2 * (cap - LANES)), BF16),
            vmem((total, width, LANES), BF16),
            vmem((nz, width, 2 * LANES), BF16),
            vmem((channels, 2 * LANES), BF16),
            vmem((channels, 2 * (cap - LANES)), BF16),
            vmem((channels, LANES), BF16),
            vmem((channels, 2 * LANES), BF16),
            vmem((channels, channels), BF16),
            vmem((channels, channels), BF16),
            vmem((64, channels), F32),
            vmem((64, channels), F32),
            vmem((16, channels), F32),
            vmem((16, channels), F32),
            vmem((2 * held, 2 * LANES), BF16),
            vmem((2 * held, 2 * (cap - LANES)), BF16),
            vmem((2 * held, LANES), BF16),
            vmem((2 * held, 2 * LANES), BF16),
            vmem((8, LANES), F32),
            vmem((3, held, LANES), jnp.int32),
            vmem((3, half, LANES), F32),
            vmem((channels, LANES), F32),
            vmem(share, BF16),
            vmem(share, BF16),
            vmem((nl,) + share[1:], BF16),
            vmem((nl, held, part), F32),
            vmem((16, LANES), BF16),
            vmem((nl, 16, LANES), BF16),
            dma(()),
            dma((4,)),
            dma(()),
            dma(()),
            dma(()),
            dma(()),
            dma(()),
            dma((nx,)),
            dma(()),
            dma((nz,)),
            dma(()),
            dma(()),
            dma(()),
            dma(()),
            dma(()),
            dma(()),
        ],
        compiler_params=pltpu.CompilerParams(
            collective_id=collective_id, has_side_effects=True, vmem_limit_bytes=60 * 2**20
        ),
    )(lst_bin, owner, size, vis, cov)


def solution(mesh):
    nl, total = mesh.shape["lst"], mesh.shape["chan"]
    nx = total // 8
    nz = total // nx

    def shards(visibility, inverse_cov, group_size, group_owner, lst_bin):
        groups, width = visibility.shape[2], visibility.shape[4]
        channels = inverse_cov.shape[0]
        held = groups // total
        sizes = (nx, nz, nl, held, channels, width)
        vis = jnp.transpose(visibility, (0, 1, 3, 4, 2)).reshape(2 * SLOT * width, groups)
        owner = group_owner.reshape(1, groups)
        size = group_size.reshape(1, groups)
        full = SLOT * held
        tight = full // 2
        fits = pl.pallas_call(
            functools.partial(fits_kernel, tight + held, LANES, sizes),
            out_shape=jax.ShapeDtypeStruct((1,), jnp.int32),
            out_specs=pl.BlockSpec(memory_space=pltpu.SMEM),
        )(owner, size)
        return lax.cond(
            fits[0] > 0,
            functools.partial(cross_power, tight, 0, sizes),
            functools.partial(cross_power, full, 1, sizes),
            lst_bin, owner, size, vis, inverse_cov,
        )

    placed = (P(None, "lst", None, None, "chan"), P(), P(), P(), P("lst"))
    return jax.shard_map(
        shards, mesh=mesh, in_specs=placed, out_specs=P(None, "chan", "lst"), check_vma=False
    )
```

```python
import functools
import math

import jax
import jax.numpy as jnp
from jax import lax
from jax.experimental import pallas as pl
from jax.experimental.pallas import tpu as pltpu
from jax.sharding import PartitionSpec as P

NBIN = 8
SLOT = 8
MESH = pl.DeviceIdType.MESH
F32 = jnp.float32
BF16 = jnp.bfloat16
NN = (((1,), (0,)), ((), ()))
NT = (((1,), (1,)), ((), ()))
TN = (((0,), (0,)), ((), ()))
TAIL = 16
LANES = 128


def dot(a, b, dims=NN):
    return lax.dot_general(a, b, dims, preferred_element_type=F32)


def one_if(condition):
    return jnp.where(condition, 1.0, 0.0).astype(BF16)


def fits_kernel(base, room, sizes, owner_ref, size_ref, out_ref):
    nx, nz, nl, held, channels, width = sizes
    first = lax.broadcasted_iota(jnp.int32, (nx * nz, 1), 0) * held
    owner = owner_ref[...]
    mine = (owner >= first) & (owner < first + held)
    lives = jnp.sum(jnp.where(mine, size_ref[...], 0), axis=1, keepdims=True)
    over = jnp.maximum(lives - base, 0).reshape(nx, nz, 1)
    out_ref[0] = jnp.where(jnp.max(jnp.sum(over, axis=0)) <= room, 1, 0)


def kernel(
    cap,
    sizes,
    bin_ref,
    owner_ref,
    size_ref,
    vis_hbm,
    cov_hbm,
    out_ref,
    vis,
    vis_sem,
    cov,
    pick,
    chosen,
    gathered,
    paired,
    send_h,
    send_a,
    send_b,
    send_p,
    rows_h,
    rows_a,
    rows_b,
    rows_p,
    table,
    fold,
    step_cos,
    step_sin,
    base_cos,
    base_sin,
    member_h,
    member_a,
    member_b,
    member_p,
    scale_ref,
    held_ref,
    sums,
    acc_b,
    share_plus,
    share_minus,
    landed,
    pieces,
    bin_send,
    bin_land,
    cov_sem,
    own_sem,
    h_send,
    h_recv,
    a_send,
    a_recv,
    b_send,
    b_recv,
    p_send,
    p_recv,
    f_send,
    f_recv,
    y_send,
    y_recv,
    n_send,
    n_recv,
):
    nx, nz, nl, held, channels, width = sizes
    half = channels // 2
    part = channels // nl
    spans = half // part
    base = cap + held
    wide = cap + 2 * LANES
    rest = cap - LANES
    lst = lax.axis_index("lst")
    chan = lax.axis_index("chan")
    x, z = chan // nz, chan % nz
    last = nz - 1
    early = 1

    def ahead(q):
        return nz // 2 + (1 - 2 * (q % 2)) * ((q + 1) // 2)

    def place(q, i):
        return lax.rem(x + i, nx) * nz + lax.rem(z + ahead(q), nz)

    def rows_of(ref, source):
        return ref.at[pl.ds(pl.multiple_of(source * width, 16), width), :]

    def h_copy(q, i):
        n = nx * q + i
        return pltpu.make_async_remote_copy(
            src_ref=send_h.at[n],
            dst_ref=rows_of(rows_h, chan),
            send_sem=h_send,
            recv_sem=h_recv,
            device_id=(lst, place(q, i)),
            device_id_type=MESH,
        )

    def a_copy(q, i):
        n = nx * q + i
        return pltpu.make_async_remote_copy(
            src_ref=send_a.at[n],
            dst_ref=rows_of(rows_a, chan),
            send_sem=a_send,
            recv_sem=a_recv,
            device_id=(lst, place(q, i)),
            device_id_type=MESH,
        )

    def b_copy(q, i):
        n = nx * q + i
        return pltpu.make_async_remote_copy(
            src_ref=send_b.at[n],
            dst_ref=rows_of(rows_b, chan),
            send_sem=b_send,
            recv_sem=b_recv.at[i],
            device_id=(lst, place(q, i)),
            device_id_type=MESH,
        )

    def p_copy(q):
        return pltpu.make_async_remote_copy(
            src_ref=send_p.at[q],
            dst_ref=rows_of(rows_p, chan),
            send_sem=p_send,
            recv_sem=p_recv.at[q],
            device_id=(lst, place(q, 0)),
            device_id_type=MESH,
        )

    def f_copy(q, j):
        source = x * nz + lax.rem(z + nz - ahead(q), nz)
        return pltpu.make_async_remote_copy(
            src_ref=rows_of(rows_p, source),
            dst_ref=rows_of(rows_p, source),
            send_sem=f_send,
            recv_sem=f_recv,
            device_id=(lst, lax.rem(x + j, nx) * nz + z),
            device_id_type=MESH,
        )

    own_h = pltpu.make_async_copy(send_h.at[nx * last], rows_of(rows_h, chan), own_sem.at[3])
    own_a = pltpu.make_async_copy(send_a.at[nx * last], rows_of(rows_a, chan), own_sem.at[0])
    own_b = pltpu.make_async_copy(send_b.at[nx * last], rows_of(rows_b, chan), own_sem.at[1])
    own_p = pltpu.make_async_copy(send_p.at[last], rows_of(rows_p, chan), own_sem.at[2])
    cov_copy = pltpu.make_async_copy(cov_hbm, cov, cov_sem)

    vis_copy = pltpu.make_async_copy(vis_hbm, vis, vis_sem)
    vis_copy.start()
    barrier = pltpu.get_barrier_semaphore()
    for other in range(1, nx * nz):
        peer = lax.rem(x + other // nz, nx) * nz + lax.rem(z + other % nz, nz)
        pl.semaphore_signal(barrier, inc=1, device_id=(lst, peer), device_id_type=MESH)
    for dl in range(1, nl):
        pl.semaphore_signal(
            barrier, inc=1, device_id=(lax.rem(lst + dl, nl), chan), device_id_type=MESH
        )

    low = lax.broadcasted_iota(jnp.int32, (width, LANES), 1) < held
    lane = lax.broadcasted_iota(jnp.int32, (1, wide), 1)
    spot = lax.broadcasted_iota(jnp.int32, (held, LANES), 0).astype(F32).astype(BF16)
    row_id = lax.broadcasted_iota(jnp.int32, (nx * held, nx * held), 0)
    col_id = lax.broadcasted_iota(jnp.int32, (nx * held, nx * held), 1)
    before = one_if((row_id // held == col_id // held) & (col_id < row_id))
    one, none = jnp.ones((held, LANES), BF16), jnp.zeros((held, LANES), BF16)

    def members(start, live, pooled):
        def spread_out(member, w, offset):
            at = lax.broadcasted_iota(jnp.int32, (held, w), 1) + offset
            mine = one_if((at >= start) & (at < start + live))
            empty = jnp.zeros((held, w), BF16)
            member[pl.ds(0, held), :] = jnp.concatenate([mine, empty], axis=1)
            member[pl.ds(held, held), :] = jnp.concatenate([empty, mine], axis=1)

        spread_out(member_h, LANES, 0)
        spread_out(member_a, rest, LANES)
        at = lax.broadcasted_iota(jnp.int32, (held, LANES), 1)
        below = at < held
        near = lax.rem(at, held) + cap
        mine = (near >= start) & (near < start + live)
        member_b[pl.ds(0, held), :] = one_if(mine & below)
        member_b[pl.ds(held, held), :] = one_if(mine & jnp.logical_not(below))
        far = at + base - pooled
        mine = one_if((far >= jnp.maximum(start, base)) & (far < start + live))
        empty = jnp.zeros((held, LANES), BF16)
        member_p[pl.ds(0, held), :] = jnp.concatenate([mine, empty], axis=1)
        member_p[pl.ds(held, held), :] = jnp.concatenate([empty, mine], axis=1)
        row_id = lax.broadcasted_iota(jnp.int32, (held, LANES), 0)
        lane = lax.rem(lax.broadcasted_iota(jnp.int32, (held, LANES), 1), held)
        spread = jnp.where(row_id == lane, jnp.broadcast_to(live, (held, LANES)), 0)
        count = jnp.sum(spread.astype(F32), axis=0, keepdims=True)
        scale_ref[...] = jnp.broadcast_to(1.0 / (count * (count - 1.0)), scale_ref.shape)

    def column(q, first):
        groups = owner_ref.shape[1]
        lives = []
        for i in range(nx):
            seat = owner_ref[...] - place(q, i) * held
            seat = jnp.where((seat >= 0) & (seat < held), seat, -1).astype(F32).astype(BF16)
            sized = size_ref[...].astype(F32).astype(BF16)
            live_sum = none
            for g in range(0, groups, LANES):
                hit = jnp.broadcast_to(seat[:, g : g + LANES], (held, LANES)) == spot
                pick[pl.ds(i * held, held), pl.ds(g, LANES)] = jnp.where(hit, one, none)
                sizes_here = jnp.broadcast_to(sized[:, g : g + LANES], (held, LANES))
                live_sum += jnp.where(hit, sizes_here, none)
            lives.append(jnp.sum(live_sum.astype(F32), axis=1, keepdims=True))
        live = jnp.concatenate(lives, axis=0)
        if not first:
            for i in range(nx - 1):

                @pl.when(q > 1)
                def _():
                    h_copy(q - 1, i).start()

            h_copy(q - 1, nx - 1).start()
            p_copy(q - 1).start()

            @pl.when(q <= early)
            def _():
                for i in range(nx):
                    a_copy(q - 1, i).start()

        live_wide = jnp.broadcast_to(live, (nx * held, LANES)).astype(BF16)
        start = dot(before, live_wide)[:, :1].astype(jnp.int32)
        live = live.astype(jnp.int32)
        if first:
            vis_copy.wait()
            cov_copy.start()
        gathered[...] = dot(vis[...], pick[...], NT)
        for i in range(nx):
            for c in range(2):
                for pair in range(SLOT // 2):
                    r0 = (c * SLOT + 2 * pair) * width
                    lanes = pl.ds((i // 2) * LANES, LANES)
                    left = gathered[pl.ds(r0, width), lanes]
                    right = gathered[pl.ds(r0 + width, width), lanes]
                    if i % 2 == 0:
                        joined = jnp.where(low, left, pltpu.roll(right, held, 1))
                    else:
                        joined = jnp.where(low, pltpu.roll(left, held, 1), right)
                    paired[i, pl.ds(c * width, width), pl.ds(pair * LANES, LANES)] = (
                        joined.astype(BF16)
                    )
        ends = (start + live).reshape(nx, held, 1)
        over = [jnp.maximum(ends[i, held - 1 : held] - base, 0) for i in range(nx)]
        pool = None
        for i in range(nx):
            pooled = jnp.zeros((1, 1), jnp.int32)
            for j in range(nx):
                if j != i:
                    ahead_of = lax.rem(x + j, nx) < lax.rem(x + i, nx)
                    pooled += jnp.where(ahead_of, over[j], 0)
            live_i = live[i * held : (i + 1) * held]
            start_i = start[i * held : (i + 1) * held]
            far = lane - (cap + LANES)
            far = jnp.where(far >= pooled, far - pooled + base, -1)
            rank = jnp.where(lane < cap + LANES, jnp.where(lane < base, lane, -1), far)
            slot = rank - start_i
            slot = jnp.where((slot < live_i) & (rank >= 0), slot, -1).astype(F32).astype(BF16)
            for s in range(SLOT):
                chosen[i, pl.ds(s * held, held), :] = jnp.where(
                    slot == float(s), jnp.ones_like(slot), jnp.zeros_like(slot)
                )
            block = dot(paired[i], chosen[i])
            if i == 0:
                held_ref[0] = jnp.broadcast_to(live_i, (held, LANES))
                held_ref[1] = jnp.broadcast_to(start_i, (held, LANES))
                held_ref[2] = jnp.broadcast_to(pooled, (held, LANES))
            n = nx * q + i
            send_h[n, :, pl.ds(0, LANES)] = block[:width, :LANES].astype(BF16)
            send_h[n, :, pl.ds(LANES, LANES)] = block[width:, :LANES].astype(BF16)
            send_a[n, :, pl.ds(0, rest)] = block[:width, LANES:cap].astype(BF16)
            send_a[n, :, pl.ds(rest, rest)] = block[width:, LANES:cap].astype(BF16)
            re, im = block[:width, cap : cap + LANES], block[width:, cap : cap + LANES]
            send_b[n] = jnp.where(low, re, pltpu.roll(im, held, 1)).astype(BF16)
            extra = block[:, cap + LANES :]
            pool = extra if pool is None else pool + extra
        send_p[q, :, pl.ds(0, LANES)] = pool[:width].astype(BF16)
        send_p[q, :, pl.ds(LANES, LANES)] = pool[width:].astype(BF16)

    column(0, True)
    pl.semaphore_wait(barrier, nx * nz - 1 + nl - 1)
    for i in range(nx - 1):
        h_copy(0, i).start()

    def later(q, carry):
        column(q, False)
        return carry

    lax.fori_loop(1, nz, later, 0)
    bin_send[...] = jnp.full(bin_send.shape, bin_ref[0], jnp.int32).astype(F32).astype(BF16)
    for i in range(1, nx):
        h_copy(last, i).start()
    own_h.start()
    own_a.start()
    own_b.start()
    own_p.start()

    def await_all(like, semaphore):
        pltpu.make_async_copy(like, like, semaphore).wait()

    blocks = nx * nz - 1
    def second_rows(q, carry):
        for i in range(nx):
            a_copy(q, i).start()
        return carry

    lax.fori_loop(early, last, second_rows, 0)
    for i in range(1, nx):
        a_copy(last, i).start()
    for i in (1, 2, 3, 0):

        def start_b(q, carry):
            b_copy(q, i).start()
            return carry

        lax.fori_loop(0, nz - (i == 0), start_b, 0)
    members(held_ref[1][:, :1], held_ref[0][:, :1], held_ref[2][:1, :1])

    def bin_copy(dl):
        return pltpu.make_async_remote_copy(
            src_ref=bin_send,
            dst_ref=bin_land.at[lst],
            send_sem=n_send,
            recv_sem=n_recv,
            device_id=(lax.rem(lst + dl, nl), chan),
            device_id_type=MESH,
        )

    for dl in range(1, nl):
        bin_copy(dl).start()
    bin_land[lst] = bin_send[...]

    steps = step_cos.shape[0]
    bases = half // steps
    unit = 2.0 * math.pi / channels
    shape = (16, channels)
    bit = lax.broadcasted_iota(jnp.int32, shape, 0)
    f = lax.broadcasted_iota(jnp.int32, shape, 1).astype(F32)
    power = jnp.zeros(shape, F32)
    for n in range(10):
        power = jnp.where(bit == n, float(2**n), power)
    product = power * f
    angle = (product - jnp.floor(product * (1.0 / channels)) * channels) * unit
    bit_cos, bit_sin = jnp.cos(angle), jnp.sin(angle)
    shape = (8, channels)
    within = lax.broadcasted_iota(jnp.int32, shape, 0)

    def turned_by(v, n):
        c, s = bit_cos[n : n + 1], bit_sin[n : n + 1]
        return v[0] * c - v[1] * s, v[1] * c + v[0] * s

    def eight(low_bit, v):
        for n in range(3):
            w = turned_by(v, low_bit + n)
            on = (within // 2**n) % 2 == 1
            v = tuple(jnp.where(on, new, old) for new, old in zip(w, v))
        return v

    tiles = [eight(0, (jnp.ones(shape, F32), jnp.zeros(shape, F32)))]
    for n in range(3, 6):
        tiles += [turned_by(v, n) for v in tiles]
    for n, v in enumerate(tiles):
        step_cos[pl.ds(8 * n, 8), :], step_sin[pl.ds(8 * n, 8), :] = v
    f = f[:8] * unit
    taper = (
        0.35875
        - 0.48829 * bit_cos[:1]
        + 0.14128 * bit_cos[1:2]
        - 0.01168 * jnp.cos(3.0 * f)[:1]
    ) * (2.0 / math.sqrt(channels))
    v = eight(6, (jnp.broadcast_to(taper, shape), jnp.zeros(shape, F32)))
    base_cos[pl.ds(0, 8), :], base_sin[pl.ds(0, 8), :] = v
    base_cos[pl.ds(8, 8), :], base_sin[pl.ds(8, 8), :] = turned_by(v, 9)
    channel = lax.broadcasted_iota(jnp.int32, (1, channels), 1)
    middle = taper * jnp.where(channel % 2 == 0, 1.0, -1.0)
    step_row = lax.broadcasted_iota(jnp.int32, (steps, channels), 0)

    def tables(a, carry):
        bc, bs = base_cos[pl.ds(a, 1), :], base_sin[pl.ds(a, 1), :]
        uc, us = step_cos[...], step_sin[...]
        at = pl.multiple_of(a * steps, steps)
        table[pl.ds(at, steps), :] = (uc * bc - us * bs).astype(BF16)
        sines = jnp.where(step_row + at == 0, middle, us * bc + uc * bs)
        table[pl.ds(half + at, steps), :] = sines.astype(BF16)
        return carry

    lax.fori_loop(0, bases, tables, 0)
    cov_copy.wait()
    tall = 256

    def folding(i, carry):
        at = pl.ds(pl.multiple_of(i * tall, tall), tall)
        fold[at, :] = dot(table[at, :], cov[...]).astype(BF16)
        return carry

    folds = channels // tall
    ahead_folds = 1
    lax.fori_loop(0, ahead_folds, folding, 0)

    def pass_on(q):
        for j in range(1, nx):
            f_copy(q, j).start()

    def folding_on(i, carry):
        q = 2 * (i - ahead_folds)
        p_copy(q).wait_recv()
        pass_on(q)

        @pl.when(q + 1 < last)
        def _():
            p_copy(q + 1).wait_recv()

        @pl.when(q + 1 == last)
        def _():
            own_p.wait()

        pass_on(q + 1)
        return folding(i, carry)

    passed = ahead_folds + nz // 2
    lax.fori_loop(ahead_folds, passed, folding_on, 0)
    lax.fori_loop(passed, folds, folding, 0)

    def swap(v, w):
        if w < LANES:
            return pltpu.roll(v, w, 1)
        return jnp.concatenate([v[:, w:], v[:, :w]], axis=1)

    def partial(h, rows, member, w):
        at = h * part if isinstance(h, int) else pl.multiple_of(h * part, part)
        if rows is None:
            c = acc_b[pl.ds(at, part), :]
            s = acc_b[pl.ds(half + at, part), :]
        else:
            c = dot(fold[pl.ds(at, part), :], rows[...])
            s = dot(fold[pl.ds(half + at, part), :], rows[...])
        first = lax.broadcasted_iota(jnp.int32, (part, 1), 0) + at == 0
        mine = member[...]

        def total(v):
            return dot(v, mine, NT)

        def exact(v):
            top = v.astype(BF16)
            return total(top) + total((v - top.astype(F32)).astype(BF16))

        if w < LANES:
            cr, sr = swap(c, w), swap(s, w)
            even, odd = c * c + cr * cr, s * s + sr * sr
            cross = 2.0 * (c * sr - cr * s)
            lane = lax.broadcasted_iota(jnp.int32, (1, 2 * w), 1)
            powers = jnp.where(first, jnp.where(lane < w, even, odd), even + odd + cross)
        else:
            rc, ic, rs, im = c[:, :w], c[:, w:], s[:, :w], s[:, w:]
            even, odd = rc * rc + ic * ic, rs * rs + im * im
            cross = 2.0 * (rc * im - ic * rs)
            powers = jnp.concatenate(
                [jnp.where(first, even, even + odd + cross), jnp.where(first, odd, even + odd - cross)],
                axis=1,
            )
        return exact(c), exact(s), total(powers.astype(BF16)), first

    own_h.wait()
    await_all(send_h.at[pl.ds(0, blocks)], h_recv)

    def part_h(h, carry):
        at = pl.ds(pl.multiple_of(h * part, part), part)
        for n, v in enumerate(partial(h, rows_h, member_h, LANES)[:3]):
            sums[n, at, :] = v
        return carry

    lax.fori_loop(0, spans, part_h, 0)
    relayed = rows_p.at[pl.ds(0, nz * (nx - 1) * width), :]
    await_all(relayed, f_recv)

    def part_p(h, carry):
        at = pl.ds(pl.multiple_of(h * part, part), part)
        for n, v in enumerate(partial(h, rows_p, member_p, LANES)[:3]):
            sums[n, at, :] += v
        return carry

    lax.fori_loop(0, spans, part_p, 0)
    own_a.wait()
    await_all(send_a.at[pl.ds(0, blocks)], a_recv)

    def part_a(h, carry):
        at = pl.ds(pl.multiple_of(h * part, part), part)
        for n, v in enumerate(partial(h, rows_a, member_a, rest)[:3]):
            sums[n, at, :] += v
        return carry

    lax.fori_loop(0, spans, part_a, 0)
    await_all(send_h.at[pl.ds(0, blocks)], h_send)
    await_all(send_a.at[pl.ds(0, blocks)], a_send)
    await_all(send_p.at[pl.ds(0, last)], p_send)
    await_all(relayed, f_send)
    await_all(bin_land.at[pl.ds(0, nl - 1)], n_send)
    await_all(bin_land.at[pl.ds(0, nl - 1)], n_recv)
    deep = nz * width
    for i in (1, 2, 3, 0):
        await_all(send_b.at[pl.ds(0, nz - (i == 0))], b_recv.at[i])
        if i == 0:
            own_b.wait()
        ch = pl.ds(pl.multiple_of(lax.rem(x + nx - i, nx) * deep, deep), deep)
        term = dot(fold[:, ch], rows_b[ch, :])
        if i == 1:
            acc_b[...] = term
        else:
            acc_b[...] += term

    def share_copy(source, h, to, dl):
        return pltpu.make_async_remote_copy(
            src_ref=source.at[h],
            dst_ref=landed.at[lst],
            send_sem=y_send,
            recv_sem=y_recv.at[dl],
            device_id=(to, chan),
            device_id_type=MESH,
        )

    def share(source, h, to):
        @pl.when(to != lst)
        def _():
            share_copy(source, h, to, lax.rem(to - lst + nl, nl)).start()

        @pl.when(to == lst)
        def _():
            landed[lst] = source[h]

    tall_share = part // 2
    below = lax.broadcasted_iota(jnp.int32, (part, LANES), 1) < held
    for h in range(spans):
        share_plus[h, pl.ds(tall_share, TAIL), :] = jnp.zeros((TAIL, LANES), BF16)

    def finish(h):
        at = pl.ds(h * part, part)
        c, s, p, first = partial(h, None, member_b, held)
        c, s, p = c + sums[0, at, :], s + sums[1, at, :], p + sums[2, at, :]
        turned = jnp.where(below, 1.0, -1.0) * pltpu.roll(s, held, 1)
        up = jnp.where(first, c, c + turned)
        down = jnp.where(first, s, c - turned)
        up, down = up * up, down * down
        whole = jnp.where(below, up + pltpu.roll(up, held, 1), down + pltpu.roll(down, held, 1))
        crossed = (whole - p) * scale_ref[:1, :]
        top, bottom = crossed[:tall_share], crossed[tall_share:]
        under = below[:tall_share]
        share_plus[h, pl.ds(0, tall_share), :] = jnp.where(
            under, top, pltpu.roll(bottom, held, 1)
        ).astype(BF16)
        minus = jnp.where(under, pltpu.roll(top, held, 1), bottom).astype(BF16)
        share_minus[h, pl.ds(0, tall_share), :] = minus

        share_minus[(h - 1) % spans, pl.ds(tall_share, TAIL), :] = minus[:TAIL]

    for h in range(spans):
        if h == 2:
            share(share_plus, 0, 0)
            share(share_plus, 1, 1)
            share(share_minus, 0, nl - 1)
        if h > 2:
            share(share_plus, h - 1, h - 1)
            share(share_minus, h - 2, nl + 1 - h)
        finish(h)
    share(share_plus, spans - 1, spans - 1)
    for h in range(spans - 2, spans):
        share(share_minus, h, nl - 1 - h)

    row = lax.broadcasted_iota(jnp.int32, (tall_share + TAIL, part), 0)
    col = lax.broadcasted_iota(jnp.int32, (tall_share + TAIL, part), 1)
    want = jnp.where(lst < spans, col, part - col)
    lower = one_if((row == want) & (row < tall_share) | (row == want - tall_share) & (want == part))
    upper = one_if((row + tall_share == want) & (row < tall_share))
    turn = jnp.concatenate([lower, upper], axis=1)

    def order(t):
        both = dot(landed[t], turn, TN)
        pieces[t] = both[:held, :part] + both[held:, part:]

    await_all(send_b.at[pl.ds(0, blocks)], b_send)
    order(lst)
    for dl in sorted(range(1, nl), key=lambda d: min(d, nl - d)):
        await_all(landed.at[0], y_recv.at[dl])
        order(lax.rem(lst + nl - dl, nl))
    codes = [bin_land[t].astype(F32)[:1, :1] for t in range(nl)]
    for b in range(NBIN):
        total = jnp.zeros((held, part), F32)
        count = jnp.zeros((1, 1), F32)
        for t in range(nl):
            inside = codes[t] == b
            total += jnp.where(inside, pieces[t], 0.0)
            count += jnp.where(inside, 1.0, 0.0)
        out_ref[b] = total * (1.0 / jnp.maximum(count, 1.0))

    await_all(landed.at[pl.ds(0, nl - 1)], y_send)


def cross_power(cap, collective_id, sizes, lst_bin, owner, size, vis, cov):
    nx, nz, nl, held, channels, width = sizes
    half = channels // 2
    part = channels // nl
    total = nx * nz
    vmem = pltpu.VMEM
    dma = pltpu.SemaphoreType.DMA
    share = (channels // (2 * part), part // 2 + TAIL, LANES)
    return pl.pallas_call(
        functools.partial(kernel, cap, sizes),
        out_shape=jax.ShapeDtypeStruct((NBIN, held, part), F32),
        in_specs=[
            pl.BlockSpec(memory_space=pltpu.SMEM),
            pl.BlockSpec(memory_space=vmem),
            pl.BlockSpec(memory_space=vmem),
            pl.BlockSpec(memory_space=pl.ANY),
            pl.BlockSpec(memory_space=pl.ANY),
        ],
        out_specs=pl.BlockSpec(memory_space=vmem),
        scratch_shapes=[
            vmem(vis.shape, BF16),
            dma(()),
            vmem((channels, channels), BF16),
            vmem((nx * held, owner.shape[1]), BF16),
            vmem((nx, SLOT * held, cap + 2 * LANES), BF16),
            vmem((2 * SLOT * width, nx * held), F32),
            vmem((nx, 2 * width, SLOT * held), BF16),
            vmem((total, width, 2 * LANES), BF16),
            vmem((total, width, 2 * (cap - LANES)), BF16),
            vmem((total, width, LANES), BF16),
            vmem((nz, width, 2 * LANES), BF16),
            vmem((channels, 2 * LANES), BF16),
            vmem((channels, 2 * (cap - LANES)), BF16),
            vmem((channels, LANES), BF16),
            vmem((channels, 2 * LANES), BF16),
            vmem((channels, channels), BF16),
            vmem((channels, channels), BF16),
            vmem((64, channels), F32),
            vmem((64, channels), F32),
            vmem((16, channels), F32),
            vmem((16, channels), F32),
            vmem((2 * held, 2 * LANES), BF16),
            vmem((2 * held, 2 * (cap - LANES)), BF16),
            vmem((2 * held, LANES), BF16),
            vmem((2 * held, 2 * LANES), BF16),
            vmem((8, LANES), F32),
            vmem((3, held, LANES), jnp.int32),
            vmem((3, half, LANES), F32),
            vmem((channels, LANES), F32),
            vmem(share, BF16),
            vmem(share, BF16),
            vmem((nl,) + share[1:], BF16),
            vmem((nl, held, part), F32),
            vmem((16, LANES), BF16),
            vmem((nl, 16, LANES), BF16),
            dma(()),
            dma((4,)),
            dma(()),
            dma(()),
            dma(()),
            dma(()),
            dma(()),
            dma((nx,)),
            dma(()),
            dma((nz,)),
            dma(()),
            dma(()),
            dma(()),
            dma((nl,)),
            dma(()),
            dma(()),
        ],
        compiler_params=pltpu.CompilerParams(
            collective_id=collective_id, has_side_effects=True, vmem_limit_bytes=60 * 2**20
        ),
    )(lst_bin, owner, size, vis, cov)


def solution(mesh):
    nl, total = mesh.shape["lst"], mesh.shape["chan"]
    nx = total // 8
    nz = total // nx

    def shards(visibility, inverse_cov, group_size, group_owner, lst_bin):
        groups, width = visibility.shape[2], visibility.shape[4]
        channels = inverse_cov.shape[0]
        held = groups // total
        sizes = (nx, nz, nl, held, channels, width)
        vis = jnp.transpose(visibility, (0, 1, 3, 4, 2)).reshape(2 * SLOT * width, groups)
        owner = group_owner.reshape(1, groups)
        size = group_size.reshape(1, groups)
        full = SLOT * held
        tight = full // 2
        fits = pl.pallas_call(
            functools.partial(fits_kernel, tight + held, LANES, sizes),
            out_shape=jax.ShapeDtypeStruct((1,), jnp.int32),
            out_specs=pl.BlockSpec(memory_space=pltpu.SMEM),
        )(owner, size)
        return lax.cond(
            fits[0] > 0,
            functools.partial(cross_power, tight, 0, sizes),
            functools.partial(cross_power, full, 1, sizes),
            lst_bin, owner, size, vis, inverse_cov,
        )

    placed = (P(None, "lst", None, None, "chan"), P(), P(), P(), P("lst"))
    return jax.shard_map(
        shards, mesh=mesh, in_specs=placed, out_specs=P(None, "chan", "lst"), check_vma=False
    )
```

```python
import functools
import math

import jax
import jax.numpy as jnp
from jax import lax
from jax.experimental import pallas as pl
from jax.experimental.pallas import tpu as pltpu
from jax.sharding import PartitionSpec as P

NBIN = 8
SLOT = 8
MESH = pl.DeviceIdType.MESH
F32 = jnp.float32
BF16 = jnp.bfloat16
NN = (((1,), (0,)), ((), ()))
NT = (((1,), (1,)), ((), ()))
TN = (((0,), (0,)), ((), ()))
TAIL = 16
LANES = 128


def dot(a, b, dims=NN):
    return lax.dot_general(a, b, dims, preferred_element_type=F32)


def one_if(condition):
    return jnp.where(condition, 1.0, 0.0).astype(BF16)


def fits_kernel(base, room, sizes, owner_ref, size_ref, out_ref):
    nx, nz, nl, held, channels, width = sizes
    first = lax.broadcasted_iota(jnp.int32, (nx * nz, 1), 0) * held
    owner = owner_ref[...]
    mine = (owner >= first) & (owner < first + held)
    lives = jnp.sum(jnp.where(mine, size_ref[...], 0), axis=1, keepdims=True)
    over = jnp.maximum(lives - base, 0).reshape(nx, nz, 1)
    out_ref[0] = jnp.where(jnp.max(jnp.sum(over, axis=0)) <= room, 1, 0)


def kernel(
    cap,
    sizes,
    bin_ref,
    owner_ref,
    size_ref,
    vis_hbm,
    cov_hbm,
    out_ref,
    vis,
    vis_sem,
    cov,
    pick,
    chosen,
    gathered,
    paired,
    send_h,
    send_a,
    send_b,
    send_p,
    rows_h,
    rows_a,
    rows_b,
    rows_p,
    table,
    fold,
    step_cos,
    step_sin,
    base_cos,
    base_sin,
    member_h,
    member_a,
    member_b,
    member_p,
    scale_ref,
    held_ref,
    sums,
    acc_b,
    share_plus,
    share_minus,
    landed,
    pieces,
    bin_send,
    bin_land,
    cov_sem,
    own_sem,
    h_send,
    h_recv,
    a_send,
    a_recv,
    b_send,
    b_recv,
    p_send,
    p_recv,
    f_send,
    f_recv,
    y_send,
    y_recv,
    n_send,
    n_recv,
):
    nx, nz, nl, held, channels, width = sizes
    half = channels // 2
    part = channels // nl
    spans = half // part
    base = cap + held
    wide = cap + 2 * LANES
    rest = cap - LANES
    lst = lax.axis_index("lst")
    chan = lax.axis_index("chan")
    x, z = chan // nz, chan % nz
    last = nz - 1
    early = 1

    def ahead(q):
        return nz // 2 + (1 - 2 * (q % 2)) * ((q + 1) // 2)

    def place(q, i):
        return lax.rem(x + i, nx) * nz + lax.rem(z + ahead(q), nz)

    def rows_of(ref, source):
        return ref.at[pl.ds(pl.multiple_of(source * width, 16), width), :]

    def h_copy(q, i):
        n = nx * q + i
        return pltpu.make_async_remote_copy(
            src_ref=send_h.at[n],
            dst_ref=rows_of(rows_h, chan),
            send_sem=h_send,
            recv_sem=h_recv,
            device_id=(lst, place(q, i)),
            device_id_type=MESH,
        )

    def a_copy(q, i):
        n = nx * q + i
        return pltpu.make_async_remote_copy(
            src_ref=send_a.at[n],
            dst_ref=rows_of(rows_a, chan),
            send_sem=a_send,
            recv_sem=a_recv,
            device_id=(lst, place(q, i)),
            device_id_type=MESH,
        )

    def b_copy(q, i):
        n = nx * q + i
        return pltpu.make_async_remote_copy(
            src_ref=send_b.at[n],
            dst_ref=rows_of(rows_b, chan),
            send_sem=b_send,
            recv_sem=b_recv.at[i],
            device_id=(lst, place(q, i)),
            device_id_type=MESH,
        )

    def p_copy(q):
        return pltpu.make_async_remote_copy(
            src_ref=send_p.at[q],
            dst_ref=rows_of(rows_p, chan),
            send_sem=p_send,
            recv_sem=p_recv.at[q],
            device_id=(lst, place(q, 0)),
            device_id_type=MESH,
        )

    def f_copy(q, j):
        source = x * nz + lax.rem(z + nz - ahead(q), nz)
        return pltpu.make_async_remote_copy(
            src_ref=rows_of(rows_p, source),
            dst_ref=rows_of(rows_p, source),
            send_sem=f_send,
            recv_sem=f_recv,
            device_id=(lst, lax.rem(x + j, nx) * nz + z),
            device_id_type=MESH,
        )

    own_h = pltpu.make_async_copy(send_h.at[nx * last], rows_of(rows_h, chan), own_sem.at[3])
    own_a = pltpu.make_async_copy(send_a.at[nx * last], rows_of(rows_a, chan), own_sem.at[0])
    own_b = pltpu.make_async_copy(send_b.at[nx * last], rows_of(rows_b, chan), own_sem.at[1])
    own_p = pltpu.make_async_copy(send_p.at[last], rows_of(rows_p, chan), own_sem.at[2])
    cov_copy = pltpu.make_async_copy(cov_hbm, cov, cov_sem)

    vis_copy = pltpu.make_async_copy(vis_hbm, vis, vis_sem)
    vis_copy.start()
    barrier = pltpu.get_barrier_semaphore()
    for other in range(1, nx * nz):
        peer = lax.rem(x + other // nz, nx) * nz + lax.rem(z + other % nz, nz)
        pl.semaphore_signal(barrier, inc=1, device_id=(lst, peer), device_id_type=MESH)
    for dl in range(1, nl):
        pl.semaphore_signal(
            barrier, inc=1, device_id=(lax.rem(lst + dl, nl), chan), device_id_type=MESH
        )

    low = lax.broadcasted_iota(jnp.int32, (width, LANES), 1) < held
    lane = lax.broadcasted_iota(jnp.int32, (1, wide), 1)
    spot = lax.broadcasted_iota(jnp.int32, (held, LANES), 0).astype(F32).astype(BF16)
    row_id = lax.broadcasted_iota(jnp.int32, (nx * held, nx * held), 0)
    col_id = lax.broadcasted_iota(jnp.int32, (nx * held, nx * held), 1)
    before = one_if((row_id // held == col_id // held) & (col_id < row_id))
    one, none = jnp.ones((held, LANES), BF16), jnp.zeros((held, LANES), BF16)

    def members(start, live, pooled):
        def spread_out(member, w, offset):
            at = lax.broadcasted_iota(jnp.int32, (held, w), 1) + offset
            mine = one_if((at >= start) & (at < start + live))
            empty = jnp.zeros((held, w), BF16)
            member[pl.ds(0, held), :] = jnp.concatenate([mine, empty], axis=1)
            member[pl.ds(held, held), :] = jnp.concatenate([empty, mine], axis=1)

        spread_out(member_h, LANES, 0)
        spread_out(member_a, rest, LANES)
        at = lax.broadcasted_iota(jnp.int32, (held, LANES), 1)
        below = at < held
        near = lax.rem(at, held) + cap
        mine = (near >= start) & (near < start + live)
        member_b[pl.ds(0, held), :] = one_if(mine & below)
        member_b[pl.ds(held, held), :] = one_if(mine & jnp.logical_not(below))
        far = at + base - pooled
        mine = one_if((far >= jnp.maximum(start, base)) & (far < start + live))
        empty = jnp.zeros((held, LANES), BF16)
        member_p[pl.ds(0, held), :] = jnp.concatenate([mine, empty], axis=1)
        member_p[pl.ds(held, held), :] = jnp.concatenate([empty, mine], axis=1)
        row_id = lax.broadcasted_iota(jnp.int32, (held, LANES), 0)
        lane = lax.rem(lax.broadcasted_iota(jnp.int32, (held, LANES), 1), held)
        spread = jnp.where(row_id == lane, jnp.broadcast_to(live, (held, LANES)), 0)
        count = jnp.sum(spread.astype(F32), axis=0, keepdims=True)
        scale_ref[...] = jnp.broadcast_to(1.0 / (count * (count - 1.0)), scale_ref.shape)

    def column(q, first):
        groups = owner_ref.shape[1]
        lives = []
        for i in range(nx):
            seat = owner_ref[...] - place(q, i) * held
            seat = jnp.where((seat >= 0) & (seat < held), seat, -1).astype(F32).astype(BF16)
            sized = size_ref[...].astype(F32).astype(BF16)
            live_sum = none
            for g in range(0, groups, LANES):
                hit = jnp.broadcast_to(seat[:, g : g + LANES], (held, LANES)) == spot
                pick[pl.ds(i * held, held), pl.ds(g, LANES)] = jnp.where(hit, one, none)
                sizes_here = jnp.broadcast_to(sized[:, g : g + LANES], (held, LANES))
                live_sum += jnp.where(hit, sizes_here, none)
            lives.append(jnp.sum(live_sum.astype(F32), axis=1, keepdims=True))
        live = jnp.concatenate(lives, axis=0)
        if not first:
            p_copy(q - 1).start()
            for i in range(nx - 1):

                @pl.when(q > 1)
                def _():
                    h_copy(q - 1, i).start()

            h_copy(q - 1, nx - 1).start()

            @pl.when(q <= early)
            def _():
                for i in range(nx):
                    a_copy(q - 1, i).start()

        live_wide = jnp.broadcast_to(live, (nx * held, LANES)).astype(BF16)
        start = dot(before, live_wide)[:, :1].astype(jnp.int32)
        live = live.astype(jnp.int32)
        if first:
            vis_copy.wait()
            cov_copy.start()
        gathered[...] = dot(vis[...], pick[...], NT)
        for i in range(nx):
            for c in range(2):
                for pair in range(SLOT // 2):
                    r0 = (c * SLOT + 2 * pair) * width
                    lanes = pl.ds((i // 2) * LANES, LANES)
                    left = gathered[pl.ds(r0, width), lanes]
                    right = gathered[pl.ds(r0 + width, width), lanes]
                    if i % 2 == 0:
                        joined = jnp.where(low, left, pltpu.roll(right, held, 1))
                    else:
                        joined = jnp.where(low, pltpu.roll(left, held, 1), right)
                    paired[i, pl.ds(c * width, width), pl.ds(pair * LANES, LANES)] = (
                        joined.astype(BF16)
                    )
        ends = (start + live).reshape(nx, held, 1)
        over = [jnp.maximum(ends[i, held - 1 : held] - base, 0) for i in range(nx)]
        pool = None
        for i in range(nx):
            pooled = jnp.zeros((1, 1), jnp.int32)
            for j in range(nx):
                if j != i:
                    ahead_of = lax.rem(x + j, nx) < lax.rem(x + i, nx)
                    pooled += jnp.where(ahead_of, over[j], 0)
            live_i = live[i * held : (i + 1) * held]
            start_i = start[i * held : (i + 1) * held]
            far = lane - (cap + LANES)
            far = jnp.where(far >= pooled, far - pooled + base, -1)
            rank = jnp.where(lane < cap + LANES, jnp.where(lane < base, lane, -1), far)
            slot = rank - start_i
            slot = jnp.where((slot < live_i) & (rank >= 0), slot, -1).astype(F32).astype(BF16)
            for s in range(SLOT):
                chosen[i, pl.ds(s * held, held), :] = jnp.where(
                    slot == float(s), jnp.ones_like(slot), jnp.zeros_like(slot)
                )
            block = dot(paired[i], chosen[i])
            if i == 0:
                held_ref[0] = jnp.broadcast_to(live_i, (held, LANES))
                held_ref[1] = jnp.broadcast_to(start_i, (held, LANES))
                held_ref[2] = jnp.broadcast_to(pooled, (held, LANES))
            n = nx * q + i
            send_h[n, :, pl.ds(0, LANES)] = block[:width, :LANES].astype(BF16)
            send_h[n, :, pl.ds(LANES, LANES)] = block[width:, :LANES].astype(BF16)
            send_a[n, :, pl.ds(0, rest)] = block[:width, LANES:cap].astype(BF16)
            send_a[n, :, pl.ds(rest, rest)] = block[width:, LANES:cap].astype(BF16)
            re, im = block[:width, cap : cap + LANES], block[width:, cap : cap + LANES]
            send_b[n] = jnp.where(low, re, pltpu.roll(im, held, 1)).astype(BF16)
            extra = block[:, cap + LANES :]
            pool = extra if pool is None else pool + extra
        send_p[q, :, pl.ds(0, LANES)] = pool[:width].astype(BF16)
        send_p[q, :, pl.ds(LANES, LANES)] = pool[width:].astype(BF16)

    column(0, True)
    pl.semaphore_wait(barrier, nx * nz - 1 + nl - 1)
    for i in range(nx - 1):
        h_copy(0, i).start()

    def later(q, carry):
        column(q, False)
        return carry

    lax.fori_loop(1, nz, later, 0)
    bin_send[...] = jnp.full(bin_send.shape, bin_ref[0], jnp.int32).astype(F32).astype(BF16)
    for i in range(1, nx):
        h_copy(last, i).start()
    own_h.start()
    own_a.start()
    own_b.start()
    own_p.start()

    def await_all(like, semaphore):
        pltpu.make_async_copy(like, like, semaphore).wait()

    blocks = nx * nz - 1
    def second_rows(q, carry):
        for i in range(nx):
            a_copy(q, i).start()
        return carry

    lax.fori_loop(early, last, second_rows, 0)
    for i in range(1, nx):
        a_copy(last, i).start()
    for i in (1, 2, 3, 0):

        def start_b(q, carry):
            b_copy(q, i).start()
            return carry

        lax.fori_loop(0, nz - (i == 0), start_b, 0)
    members(held_ref[1][:, :1], held_ref[0][:, :1], held_ref[2][:1, :1])

    def bin_copy(dl):
        return pltpu.make_async_remote_copy(
            src_ref=bin_send,
            dst_ref=bin_land.at[lst],
            send_sem=n_send,
            recv_sem=n_recv,
            device_id=(lax.rem(lst + dl, nl), chan),
            device_id_type=MESH,
        )

    for dl in range(1, nl):
        bin_copy(dl).start()
    bin_land[lst] = bin_send[...]

    steps = step_cos.shape[0]
    bases = half // steps
    unit = 2.0 * math.pi / channels
    shape = (16, channels)
    bit = lax.broadcasted_iota(jnp.int32, shape, 0)
    f = lax.broadcasted_iota(jnp.int32, shape, 1).astype(F32)
    power = jnp.zeros(shape, F32)
    for n in range(10):
        power = jnp.where(bit == n, float(2**n), power)
    product = power * f
    angle = (product - jnp.floor(product * (1.0 / channels)) * channels) * unit
    bit_cos, bit_sin = jnp.cos(angle), jnp.sin(angle)
    shape = (8, channels)
    within = lax.broadcasted_iota(jnp.int32, shape, 0)

    def turned_by(v, n):
        c, s = bit_cos[n : n + 1], bit_sin[n : n + 1]
        return v[0] * c - v[1] * s, v[1] * c + v[0] * s

    def eight(low_bit, v):
        for n in range(3):
            w = turned_by(v, low_bit + n)
            on = (within // 2**n) % 2 == 1
            v = tuple(jnp.where(on, new, old) for new, old in zip(w, v))
        return v

    tiles = [eight(0, (jnp.ones(shape, F32), jnp.zeros(shape, F32)))]
    for n in range(3, 6):
        tiles += [turned_by(v, n) for v in tiles]
    for n, v in enumerate(tiles):
        step_cos[pl.ds(8 * n, 8), :], step_sin[pl.ds(8 * n, 8), :] = v
    f = f[:8] * unit
    taper = (
        0.35875
        - 0.48829 * bit_cos[:1]
        + 0.14128 * bit_cos[1:2]
        - 0.01168 * jnp.cos(3.0 * f)[:1]
    ) * (2.0 / math.sqrt(channels))
    v = eight(6, (jnp.broadcast_to(taper, shape), jnp.zeros(shape, F32)))
    base_cos[pl.ds(0, 8), :], base_sin[pl.ds(0, 8), :] = v
    base_cos[pl.ds(8, 8), :], base_sin[pl.ds(8, 8), :] = turned_by(v, 9)
    channel = lax.broadcasted_iota(jnp.int32, (1, channels), 1)
    middle = taper * jnp.where(channel % 2 == 0, 1.0, -1.0)
    step_row = lax.broadcasted_iota(jnp.int32, (steps, channels), 0)

    def tables(a, carry):
        bc, bs = base_cos[pl.ds(a, 1), :], base_sin[pl.ds(a, 1), :]
        uc, us = step_cos[...], step_sin[...]
        at = pl.multiple_of(a * steps, steps)
        table[pl.ds(at, steps), :] = (uc * bc - us * bs).astype(BF16)
        sines = jnp.where(step_row + at == 0, middle, us * bc + uc * bs)
        table[pl.ds(half + at, steps), :] = sines.astype(BF16)
        return carry

    lax.fori_loop(0, bases, tables, 0)
    cov_copy.wait()
    tall = 256

    def folding(i, carry):
        at = pl.ds(pl.multiple_of(i * tall, tall), tall)
        fold[at, :] = dot(table[at, :], cov[...]).astype(BF16)
        return carry

    folds = channels // tall
    ahead_folds = 0

    def pass_on(q):
        for j in range(1, nx):
            f_copy(q, j).start()

    def folding_on(i, carry):
        q = 2 * (i - ahead_folds)
        p_copy(q).wait_recv()
        pass_on(q)

        @pl.when(q + 1 < last)
        def _():
            p_copy(q + 1).wait_recv()

        @pl.when(q + 1 == last)
        def _():
            own_p.wait()

        pass_on(q + 1)
        return folding(i, carry)

    passed = ahead_folds + nz // 2
    lax.fori_loop(ahead_folds, passed, folding_on, 0)
    lax.fori_loop(passed, folds, folding, 0)

    def swap(v, w):
        if w < LANES:
            return pltpu.roll(v, w, 1)
        return jnp.concatenate([v[:, w:], v[:, :w]], axis=1)

    def partial(h, rows, member, w):
        at = h * part if isinstance(h, int) else pl.multiple_of(h * part, part)
        if rows is None:
            c = acc_b[pl.ds(at, part), :]
            s = acc_b[pl.ds(half + at, part), :]
        else:
            c = dot(fold[pl.ds(at, part), :], rows[...])
            s = dot(fold[pl.ds(half + at, part), :], rows[...])
        first = lax.broadcasted_iota(jnp.int32, (part, 1), 0) + at == 0
        mine = member[...]

        def total(v):
            return dot(v, mine, NT)

        def exact(v):
            top = v.astype(BF16)
            return total(top) + total((v - top.astype(F32)).astype(BF16))

        if w < LANES:
            cr, sr = swap(c, w), swap(s, w)
            even, odd = c * c + cr * cr, s * s + sr * sr
            cross = 2.0 * (c * sr - cr * s)
            lane = lax.broadcasted_iota(jnp.int32, (1, 2 * w), 1)
            powers = jnp.where(first, jnp.where(lane < w, even, odd), even + odd + cross)
        else:
            rc, ic, rs, im = c[:, :w], c[:, w:], s[:, :w], s[:, w:]
            even, odd = rc * rc + ic * ic, rs * rs + im * im
            cross = 2.0 * (rc * im - ic * rs)
            powers = jnp.concatenate(
                [jnp.where(first, even, even + odd + cross), jnp.where(first, odd, even + odd - cross)],
                axis=1,
            )
        return exact(c), exact(s), total(powers.astype(BF16)), first

    own_h.wait()
    await_all(send_h.at[pl.ds(0, blocks)], h_recv)

    def part_h(h, carry):
        at = pl.ds(pl.multiple_of(h * part, part), part)
        for n, v in enumerate(partial(h, rows_h, member_h, LANES)[:3]):
            sums[n, at, :] = v
        return carry

    lax.fori_loop(0, spans, part_h, 0)
    relayed = rows_p.at[pl.ds(0, nz * (nx - 1) * width), :]
    await_all(relayed, f_recv)

    def part_p(h, carry):
        at = pl.ds(pl.multiple_of(h * part, part), part)
        for n, v in enumerate(partial(h, rows_p, member_p, LANES)[:3]):
            sums[n, at, :] += v
        return carry

    lax.fori_loop(0, spans, part_p, 0)
    own_a.wait()
    await_all(send_a.at[pl.ds(0, blocks)], a_recv)

    def part_a(h, carry):
        at = pl.ds(pl.multiple_of(h * part, part), part)
        for n, v in enumerate(partial(h, rows_a, member_a, rest)[:3]):
            sums[n, at, :] += v
        return carry

    lax.fori_loop(0, spans, part_a, 0)
    await_all(send_h.at[pl.ds(0, blocks)], h_send)
    await_all(send_a.at[pl.ds(0, blocks)], a_send)
    await_all(send_p.at[pl.ds(0, last)], p_send)
    await_all(relayed, f_send)
    await_all(bin_land.at[pl.ds(0, nl - 1)], n_send)
    await_all(bin_land.at[pl.ds(0, nl - 1)], n_recv)
    deep = nz * width
    for i in (1, 2, 3, 0):
        await_all(send_b.at[pl.ds(0, nz - (i == 0))], b_recv.at[i])
        if i == 0:
            own_b.wait()
        ch = pl.ds(pl.multiple_of(lax.rem(x + nx - i, nx) * deep, deep), deep)
        term = dot(fold[:, ch], rows_b[ch, :])
        if i == 1:
            acc_b[...] = term
        else:
            acc_b[...] += term

    def share_copy(source, h, to):
        return pltpu.make_async_remote_copy(
            src_ref=source.at[h],
            dst_ref=landed.at[lst],
            send_sem=y_send,
            recv_sem=y_recv,
            device_id=(to, chan),
            device_id_type=MESH,
        )

    def share(source, h, to):
        @pl.when(to != lst)
        def _():
            share_copy(source, h, to).start()

        @pl.when(to == lst)
        def _():
            landed[lst] = source[h]

    tall_share = part // 2
    below = lax.broadcasted_iota(jnp.int32, (part, LANES), 1) < held
    for h in range(spans):
        share_plus[h, pl.ds(tall_share, TAIL), :] = jnp.zeros((TAIL, LANES), BF16)

    def finish(h):
        at = pl.ds(h * part, part)
        c, s, p, first = partial(h, None, member_b, held)
        c, s, p = c + sums[0, at, :], s + sums[1, at, :], p + sums[2, at, :]
        turned = jnp.where(below, 1.0, -1.0) * pltpu.roll(s, held, 1)
        up = jnp.where(first, c, c + turned)
        down = jnp.where(first, s, c - turned)
        up, down = up * up, down * down
        whole = jnp.where(below, up + pltpu.roll(up, held, 1), down + pltpu.roll(down, held, 1))
        crossed = (whole - p) * scale_ref[:1, :]
        top, bottom = crossed[:tall_share], crossed[tall_share:]
        under = below[:tall_share]
        share_plus[h, pl.ds(0, tall_share), :] = jnp.where(
            under, top, pltpu.roll(bottom, held, 1)
        ).astype(BF16)
        minus = jnp.where(under, pltpu.roll(top, held, 1), bottom).astype(BF16)
        share_minus[h, pl.ds(0, tall_share), :] = minus

        share_minus[(h - 1) % spans, pl.ds(tall_share, TAIL), :] = minus[:TAIL]

    for h in range(spans):
        if h == 2:
            share(share_plus, 0, 0)
            share(share_plus, 1, 1)
            share(share_minus, 0, nl - 1)
        finish(h)
    for h in range(2, spans):
        share(share_plus, h, h)
    for h in range(1, spans):
        share(share_minus, h, nl - 1 - h)

    row = lax.broadcasted_iota(jnp.int32, (tall_share + TAIL, part), 0)
    col = lax.broadcasted_iota(jnp.int32, (tall_share + TAIL, part), 1)
    want = jnp.where(lst < spans, col, part - col)
    lower = one_if((row == want) & (row < tall_share) | (row == want - tall_share) & (want == part))
    upper = one_if((row + tall_share == want) & (row < tall_share))
    turn = jnp.concatenate([lower, upper], axis=1)

    def order(t):
        both = dot(landed[t], turn, TN)
        pieces[t] = both[:held, :part] + both[held:, part:]

    await_all(send_b.at[pl.ds(0, blocks)], b_send)
    order(lst)
    await_all(landed.at[pl.ds(0, nl - 1)], y_recv)
    for dl in range(1, nl):
        order(lax.rem(lst + dl, nl))
    codes = [bin_land[t].astype(F32)[:1, :1] for t in range(nl)]
    for b in range(NBIN):
        total = jnp.zeros((held, part), F32)
        count = jnp.zeros((1, 1), F32)
        for t in range(nl):
            inside = codes[t] == b
            total += jnp.where(inside, pieces[t], 0.0)
            count += jnp.where(inside, 1.0, 0.0)
        out_ref[b] = total * (1.0 / jnp.maximum(count, 1.0))

    await_all(landed.at[pl.ds(0, nl - 1)], y_send)


def cross_power(cap, collective_id, sizes, lst_bin, owner, size, vis, cov):
    nx, nz, nl, held, channels, width = sizes
    half = channels // 2
    part = channels // nl
    total = nx * nz
    vmem = pltpu.VMEM
    dma = pltpu.SemaphoreType.DMA
    share = (channels // (2 * part), part // 2 + TAIL, LANES)
    return pl.pallas_call(
        functools.partial(kernel, cap, sizes),
        out_shape=jax.ShapeDtypeStruct((NBIN, held, part), F32),
        in_specs=[
            pl.BlockSpec(memory_space=pltpu.SMEM),
            pl.BlockSpec(memory_space=vmem),
            pl.BlockSpec(memory_space=vmem),
            pl.BlockSpec(memory_space=pl.ANY),
            pl.BlockSpec(memory_space=pl.ANY),
        ],
        out_specs=pl.BlockSpec(memory_space=vmem),
        scratch_shapes=[
            vmem(vis.shape, BF16),
            dma(()),
            vmem((channels, channels), BF16),
            vmem((nx * held, owner.shape[1]), BF16),
            vmem((nx, SLOT * held, cap + 2 * LANES), BF16),
            vmem((2 * SLOT * width, nx * held), F32),
            vmem((nx, 2 * width, SLOT * held), BF16),
            vmem((total, width, 2 * LANES), BF16),
            vmem((total, width, 2 * (cap - LANES)), BF16),
            vmem((total, width, LANES), BF16),
            vmem((nz, width, 2 * LANES), BF16),
            vmem((channels, 2 * LANES), BF16),
            vmem((channels, 2 * (cap - LANES)), BF16),
            vmem((channels, LANES), BF16),
            vmem((channels, 2 * LANES), BF16),
            vmem((channels, channels), BF16),
            vmem((channels, channels), BF16),
            vmem((64, channels), F32),
            vmem((64, channels), F32),
            vmem((16, channels), F32),
            vmem((16, channels), F32),
            vmem((2 * held, 2 * LANES), BF16),
            vmem((2 * held, 2 * (cap - LANES)), BF16),
            vmem((2 * held, LANES), BF16),
            vmem((2 * held, 2 * LANES), BF16),
            vmem((8, LANES), F32),
            vmem((3, held, LANES), jnp.int32),
            vmem((3, half, LANES), F32),
            vmem((channels, LANES), F32),
            vmem(share, BF16),
            vmem(share, BF16),
            vmem((nl,) + share[1:], BF16),
            vmem((nl, held, part), F32),
            vmem((16, LANES), BF16),
            vmem((nl, 16, LANES), BF16),
            dma(()),
            dma((4,)),
            dma(()),
            dma(()),
            dma(()),
            dma(()),
            dma(()),
            dma((nx,)),
            dma(()),
            dma((nz,)),
            dma(()),
            dma(()),
            dma(()),
            dma(()),
            dma(()),
            dma(()),
        ],
        compiler_params=pltpu.CompilerParams(
            collective_id=collective_id, has_side_effects=True, vmem_limit_bytes=60 * 2**20
        ),
    )(lst_bin, owner, size, vis, cov)


def solution(mesh):
    nl, total = mesh.shape["lst"], mesh.shape["chan"]
    nx = total // 8
    nz = total // nx

    def shards(visibility, inverse_cov, group_size, group_owner, lst_bin):
        groups, width = visibility.shape[2], visibility.shape[4]
        channels = inverse_cov.shape[0]
        held = groups // total
        sizes = (nx, nz, nl, held, channels, width)
        vis = jnp.transpose(visibility, (0, 1, 3, 4, 2)).reshape(2 * SLOT * width, groups)
        owner = group_owner.reshape(1, groups)
        size = group_size.reshape(1, groups)
        full = SLOT * held
        tight = full // 2
        fits = pl.pallas_call(
            functools.partial(fits_kernel, tight + held, LANES, sizes),
            out_shape=jax.ShapeDtypeStruct((1,), jnp.int32),
            out_specs=pl.BlockSpec(memory_space=pltpu.SMEM),
        )(owner, size)
        return lax.cond(
            fits[0] > 0,
            functools.partial(cross_power, tight, 0, sizes),
            functools.partial(cross_power, full, 1, sizes),
            lst_bin, owner, size, vis, inverse_cov,
        )

    placed = (P(None, "lst", None, None, "chan"), P(), P(), P(), P("lst"))
    return jax.shard_map(
        shards, mesh=mesh, in_specs=placed, out_specs=P(None, "chan", "lst"), check_vma=False
    )
```
